32 devices in a mesh: row: 16 (over z, x, core), col: 2 (over y).
Axes of the slice: x: 2, y: 2, z: 4, core: 2. Of those that a mesh axis runs over, the one named last changes fastest.
Arguments:
- density_factor: bfloat16 [6144, 512], P('row', 'col'), may hold values from -0.25 to 0.25
- hole_factor: bfloat16 [6144, 512], P('row', 'col'), may hold values from -0.25 to 0.25
- ph_factor: bfloat16 [6144, 512], P('row', 'col'), may hold values from -0.25 to 0.25
- hamiltonian: bfloat16 [6144, 6144], P('row', 'col'), as said below
- multiplier_q: bfloat16 [6144, 6144], P('row', 'col'), as said below
- multiplier_g: bfloat16 [6144, 6144], P('row', 'col'), as said below
- ph_perm: int32 [6144], replicated, may hold values from 0 to 6143, as said below
- block_lengths: int32 [48], replicated, may hold values from 1 to 256, 6144 in all
Outputs:
- grad_density: float32 [6144, 512], P('row', 'col')
- grad_hole: float32 [6144, 512], P('row', 'col')
- grad_ph: float32 [6144, 512], P('row', 'col')
The draws below stay inside these ranges and needn't reach their ends.
Inputs may be any that keep to these rules, and one draw needn't show every extreme that they name: `ph_perm`: a permutation of the rows; each aligned block of 384 entries holds exactly 24 values from each aligned range of 384 rows. `block_lengths`: the lengths sum to 6144. `hamiltonian`: symmetric. `multiplier_q`: symmetric. `multiplier_g`: symmetric.
All inputs are finite; a program needn't handle non-finite values.
Results may differ from the reference program's by a relative error of at most 0.00035.
The reference program's roundings to bfloat16 on the way (of `density_ph`) count: a program that leaves them out, or rounds other values in their place, can miss the bound.
Values may be sent and summed in bfloat16 or wider, within the bound.
A program may use at most 128 MiB of HBM per device.

```python
import math
import jax
import jax.numpy as jnp
import numpy as np

NP = 6144
RANK = 512
SEGS = 48
MOSTLEN = 256
PH_BLOCK = 384
SENDS = 24


def symmetric_matrix(key, salt):
    base = jax.random.fold_in(key, salt)
    entries = jax.random.normal(jax.random.fold_in(base, 1), (NP, NP), jnp.float32)
    return ((entries + entries.T) * (0.15 / math.sqrt(2.0))).astype(jnp.bfloat16)


def draw_hamiltonian(key, part):
    return symmetric_matrix(key, 11)


def draw_multiplier_q(key, part):
    return symmetric_matrix(key, 12)


def draw_multiplier_g(key, part):
    return symmetric_matrix(key, 13)


def shuffle_block(subkey):
    return jax.random.permutation(subkey, PH_BLOCK).astype(jnp.int32)


def draw_ph_perm(key, part):
    groups = NP // PH_BLOCK
    base = jax.random.fold_in(key, 31)
    first_keys = jax.random.split(jax.random.fold_in(base, 1), groups)
    inner = jax.vmap(shuffle_block)(first_keys)
    source_rows = jnp.arange(groups, dtype=jnp.int32)[:, None] * PH_BLOCK + inner
    grouped = source_rows.reshape(groups, groups, SENDS).transpose(1, 0, 2).reshape(groups, PH_BLOCK)
    second_keys = jax.random.split(jax.random.fold_in(base, 2), groups)
    order = jax.vmap(shuffle_block)(second_keys)
    mixed = jnp.take_along_axis(grouped, order, axis=1)
    return mixed.reshape(NP).astype(jnp.int32)


def shard_levels(key, extent, cuts, smallest, top_value):
    def one(position, parts):
        heights = jax.random.uniform(jax.random.fold_in(jax.random.fold_in(key, 6), position), (parts,), jnp.float32, smallest / len(cuts), top_value / len(cuts))
        return jnp.repeat(jnp.exp(heights), extent[position] // parts).reshape((-1,) + (1,) * (len(extent) - position - 1))

    factor_of = one(*cuts[0])
    for cut in cuts[1:]:
        factor_of = factor_of * one(*cut)
    return factor_of


def profile(count, total, reach, lean):
    portions = [(1 << 20) // math.isqrt(standing ** lean) + 1 for standing in range(2, count + 1)]
    spare, counts = total - reach - (count - 1), [1] * (count - 1)
    while spare > 0:
        movable = [i for i in range(count - 1) if counts[i] < reach]
        whole, budget = sum([portions[i] for i in movable]), spare
        for i in movable:
            addition = min(reach - counts[i], max(1, budget * portions[i] // whole), spare)
            counts[i] = counts[i] + addition
            spare = spare - addition
    return np.array([reach] + counts)


def uneven_parts(stream_key, number_of, total, limit, skew):
    if number_of == 2:
        one = jax.random.randint(stream_key, (), max(1, total - limit), min(limit, total - 1) + 1)
        return jnp.stack([one, total - one])
    sizes = jnp.asarray(profile(number_of, total, limit, skew), jnp.int32)
    couples = (number_of - 1) // 2
    donor, taker = sizes[1:1 + 2 * couples:2], sizes[2:2 + 2 * couples:2]
    margin = jnp.minimum(donor - 1, limit - taker)
    moved = jax.random.randint(jax.random.fold_in(stream_key, 1), (couples,), 0, 1 << 20) % (margin + 1)
    sizes = sizes.at[1:1 + 2 * couples:2].set(donor - moved).at[2:2 + 2 * couples:2].set(taker + moved)
    return sizes[jax.random.permutation(jax.random.fold_in(stream_key, 2), number_of)]


def noise(stream_key, dims, scale, most, cuts=(), kind=jnp.bfloat16):
    values = scale * jax.random.normal(stream_key, dims, jnp.float32)
    if cuts:
        values = values * shard_levels(stream_key, dims, cuts, -0.22, 0.18)
    return jnp.clip(values, -most, most).astype(kind)


def setup_inputs(seed: int = 0) -> dict:
    splits = jax.random.split(jax.random.key(seed), 9)
    return {
        "density_factor": noise(splits[0], (NP, RANK), (RANK ** -0.5), 0.25, ((0, 16), (1, 2))),
        "hole_factor": noise(splits[1], (NP, RANK), (RANK ** -0.5), 0.25, ((0, 16), (1, 2))),
        "ph_factor": noise(splits[2], (NP, RANK), (RANK ** -0.5), 0.25, ((0, 16), (1, 2))),
        "hamiltonian": draw_hamiltonian(jax.random.fold_in(splits[8], 71), 0),
        "multiplier_q": draw_multiplier_q(jax.random.fold_in(splits[8], 71), 0),
        "multiplier_g": draw_multiplier_g(jax.random.fold_in(splits[8], 71), 0),
        "ph_perm": draw_ph_perm(jax.random.fold_in(splits[8], 71), 0),
        "block_lengths": uneven_parts(splits[7], SEGS, NP, MOSTLEN, 2).astype(jnp.int32),
    }


shift_value = 2.0
penalty = 2.5


def block_means(values, lengths):
    offsets = jnp.cumsum(lengths).astype(jnp.int32)
    positions = jnp.arange(values.shape[0], dtype=jnp.int32)
    segment = jnp.sum((positions[:, None] >= offsets[None, :]).astype(jnp.int32), axis=1).astype(jnp.int32)
    member = (segment[:, None] == jnp.arange(lengths.shape[0], dtype=jnp.int32)[None, :]).astype(values.dtype)
    means = jnp.sum(member * values[:, None], axis=0) / lengths.astype(values.dtype)
    return jnp.sum(member * means[None, :], axis=1)


def reference(density_factor, hole_factor, ph_factor, hamiltonian, multiplier_q, multiplier_g, ph_perm, block_lengths):
    density_ph = jnp.take(density_factor, ph_perm, axis=0)
    pair_cat = jnp.concatenate([density_factor, hole_factor], axis=1)
    ph_cat = jnp.concatenate([density_ph, ph_factor], axis=1)
    identity = jnp.eye(NP, dtype=jnp.float32)
    diag_density = jnp.sum(jnp.square(density_factor.astype(jnp.float32)), axis=1)
    shifted = 2.0 * block_means(diag_density, block_lengths)
    shifted_ph = jnp.take(shifted, ph_perm)
    resid_q = shift_value * identity - jnp.dot(pair_cat, pair_cat.T, preferred_element_type=jnp.float32)
    resid_g = shifted_ph[:, None] * identity - jnp.dot(ph_cat, ph_cat.T, preferred_element_type=jnp.float32)
    full_q = multiplier_q.astype(jnp.float32) + penalty * resid_q
    full_g = multiplier_g.astype(jnp.float32) + penalty * resid_g
    weight_q = full_q.astype(jnp.bfloat16)
    weight_g = full_g.astype(jnp.bfloat16)
    weight_pair = jnp.zeros((NP,), jnp.float32).at[ph_perm].set(jnp.diagonal(full_g))
    scaling = 2.0 * block_means(weight_pair, block_lengths)
    energy = jnp.dot(hamiltonian, density_factor, preferred_element_type=jnp.float32)
    pair_term = jnp.dot(weight_q, pair_cat, preferred_element_type=jnp.float32)
    ph_term = jnp.dot(weight_g, ph_cat, preferred_element_type=jnp.float32)
    returned = jnp.zeros((NP, RANK), jnp.float32).at[ph_perm].set(ph_term[:, :RANK])
    grad_density = 2.0 * energy - 2.0 * pair_term[:, :RANK] + 2.0 * scaling[:, None] * density_factor.astype(jnp.float32) - 2.0 * returned
    grad_hole = -2.0 * pair_term[:, RANK:]
    grad_ph = -2.0 * ph_term[:, RANK:]
    return (grad_density, grad_hole, grad_ph)
```

```python
import jax
import jax.numpy as jnp
from jax import lax
from jax.experimental import pallas as pl
from jax.experimental.pallas import tpu as pltpu
from jax.sharding import PartitionSpec as P

shift_value = 2.0
penalty = 2.5


def tile_weight(offset_ref, own_ref, cols_ref, mult_ref, shift):
    parts, block, _ = own_ref.shape
    tile = cols_ref.shape[1]
    gram = None
    for part in range(parts):
        term = lax.dot_general(
            own_ref[part],
            cols_ref[part],
            (((1,), (1,)), ((), ())),
            preferred_element_type=jnp.float32,
        )
        gram = term if gram is None else gram + term
    rows = lax.broadcasted_iota(jnp.int32, (block, tile), 0) + offset_ref[0]
    cols = lax.broadcasted_iota(jnp.int32, (block, tile), 1) + pl.program_id(0) * tile
    resid = jnp.where(rows == cols, shift, 0.0) - gram
    return (mult_ref[...].astype(jnp.float32) + penalty * resid).astype(jnp.bfloat16)


def pair_kernel(offset_ref, own_ref, cols_ref, mult_ref, ham_ref, out_ref):
    @pl.when(pl.program_id(0) == 0)
    def _():
        out_ref[...] = jnp.zeros_like(out_ref)

    half = own_ref.shape[2] // 2
    weight = tile_weight(offset_ref, own_ref, cols_ref, mult_ref, shift_value)
    for part in range(own_ref.shape[0]):
        first = cols_ref[part, :, :half]
        out_ref[part, :, :half] += jnp.dot(
            ham_ref[...], first, preferred_element_type=jnp.float32
        ) - jnp.dot(weight, first, preferred_element_type=jnp.float32)
        out_ref[part, :, half:] -= jnp.dot(
            weight, cols_ref[part, :, half:], preferred_element_type=jnp.float32
        )


def ph_kernel(offset_ref, own_ref, cols_ref, mult_ref, shift_ref, out_ref):
    @pl.when(pl.program_id(0) == 0)
    def _():
        out_ref[...] = jnp.zeros_like(out_ref)

    weight = tile_weight(offset_ref, own_ref, cols_ref, mult_ref, shift_ref[...])
    for part in range(own_ref.shape[0]):
        out_ref[part] -= jnp.dot(weight, cols_ref[part], preferred_element_type=jnp.float32)


def apply_weight(kernel, name, offset, own, cols, mult, extra, extra_tiled):
    parts, block, depth = own.shape
    width = cols.shape[1]
    tile = 512 if width % 512 == 0 else 256
    if extra_tiled:
        extra_spec = pl.BlockSpec((block, tile), lambda j, o: (0, j))
    else:
        extra_spec = pl.BlockSpec(extra.shape, lambda j, o: (0, 0))
    return pl.pallas_call(
        kernel,
        name=name,
        out_shape=jax.ShapeDtypeStruct((parts, block, depth), jnp.float32),
        grid_spec=pltpu.PrefetchScalarGridSpec(
            num_scalar_prefetch=1,
            grid=(width // tile,),
            in_specs=[
                pl.BlockSpec((parts, block, depth), lambda j, o: (0, 0, 0)),
                pl.BlockSpec((parts, tile, depth), lambda j, o: (0, j, 0)),
                pl.BlockSpec((block, tile), lambda j, o: (0, j)),
                extra_spec,
            ],
            out_specs=pl.BlockSpec((parts, block, depth), lambda j, o: (0, 0, 0)),
        ),
        compiler_params=pltpu.CompilerParams(
            dimension_semantics=("arbitrary",), vmem_limit_bytes=40 << 20
        ),
        cost_estimate=pl.CostEstimate(
            flops=(5 if extra_tiled else 4) * block * width * parts * depth,
            bytes_accessed=2 * width * (parts * depth + 2 * block),
            transcendentals=0,
        ),
    )(offset, own, cols, mult, extra)


def select(one_hot, values, left_axis):
    if values.dtype == jnp.float32:
        precision = lax.Precision.HIGHEST
    else:
        precision = None
    return lax.dot_general(
        one_hot.astype(values.dtype),
        values,
        (((left_axis,), (0,)), ((), ())),
        precision=precision,
        preferred_element_type=jnp.float32,
    ).astype(values.dtype)


def local(
    density_factor,
    hole_factor,
    ph_factor,
    hamiltonian,
    multiplier_q,
    multiplier_g,
    ph_perm,
    block_lengths,
):
    groups = lax.axis_size("row")
    col_groups = lax.axis_size("col")
    row_index = lax.axis_index("row")
    col_index = lax.axis_index("col")
    block, rank_part = density_factor.shape
    width = multiplier_q.shape[1]
    sends = block // groups
    per = groups // col_groups
    both = ("row", "col")

    placing = [
        (r * col_groups + c, (c * per + r % per) * col_groups + r // per)
        for r in range(groups)
        for c in range(col_groups)
    ]

    def whole_cols(piece):
        placed = lax.ppermute(piece, both, placing)
        whole = lax.all_gather(placed, "row", axis=0, tiled=True)
        return whole.reshape(col_groups, width, 2 * rank_part)

    pair_local = jnp.concatenate([density_factor, hole_factor], axis=1)
    pair_cols = whole_cols(pair_local)

    index = jnp.arange(block, dtype=jnp.int32)
    row_ids = row_index * block + index
    mine = lax.dynamic_slice_in_dim(ph_perm, row_index * block, block)
    source = mine // block
    same_source = (source[:, None] == source[None, :]) & (index[None, :] < index[:, None])
    slot = source * sends + jnp.sum(same_source.astype(jnp.int32), axis=1)
    everywhere = jnp.arange(groups * block, dtype=jnp.int32)
    inverse = jnp.sum(
        jnp.where(ph_perm[None, :] == row_ids[:, None], everywhere[None, :], 0), axis=1
    )
    target = inverse // block
    same_target = (target[:, None] == target[None, :]) & (inverse[None, :] < inverse[:, None])
    outlet = target * sends + jnp.sum(same_target.astype(jnp.int32), axis=1)
    send_hot = outlet[:, None] == index[None, :]
    take_hot = slot[:, None] == index[None, :]

    outgoing = select(send_hot, density_factor, 0)
    incoming = lax.all_to_all(outgoing, "row", split_axis=0, concat_axis=0, tiled=True)
    density_ph = select(take_hot, incoming, 1)
    ph_local = jnp.concatenate([density_ph, ph_factor], axis=1)
    ph_cols = whole_cols(ph_local)

    lengths = block_lengths.astype(jnp.float32)
    count = block_lengths.shape[0]
    upto = jnp.arange(count, dtype=jnp.int32)
    ends = jnp.sum(jnp.where(upto[None, :] <= upto[:, None], block_lengths[None, :], 0), axis=1)
    starts = ends - block_lengths

    def member_of(ids):
        inside = (ids[:, None] >= starts[None, :]) & (ids[:, None] < ends[None, :])
        return inside.astype(jnp.float32)

    member = member_of(row_ids)
    member_ph = member_of(mine)
    density_sq = jnp.sum(jnp.square(density_factor.astype(jnp.float32)), axis=1)
    ph_sq = jnp.sum(jnp.square(ph_factor.astype(jnp.float32)), axis=1)
    offset = row_index * block - col_index * width
    holds = (offset >= 0) & (offset < width)
    square = lax.dynamic_slice_in_dim(
        multiplier_g, jnp.clip(offset, 0, width - block), block, axis=1
    )
    keep = (index[:, None] == index[None, :]) & holds
    mult_diag = jnp.sum(jnp.where(keep, square.astype(jnp.float32), 0.0), axis=1)
    sums = lax.psum(
        jnp.stack(
            [
                jnp.sum(member * density_sq[:, None], axis=0),
                jnp.sum(member_ph * (mult_diag - penalty * ph_sq)[:, None], axis=0),
            ]
        ),
        both,
    )
    shift_means = 2.0 * sums[0] / lengths
    scale_means = 2.0 * (sums[1] + penalty * sums[0]) / lengths
    shift_rows = jnp.sum(member_ph * shift_means[None, :], axis=1)
    scale_rows = jnp.sum(member * scale_means[None, :], axis=1)

    pair_own = lax.all_gather(pair_local, "col", axis=0)
    ph_own = lax.all_gather(ph_local, "col", axis=0)
    offsets = offset.reshape(1)
    pair_part = apply_weight(
        pair_kernel, "pair", offsets, pair_own, pair_cols, multiplier_q, hamiltonian, True
    )
    pair_grad = lax.psum_scatter(pair_part, "col", scatter_dimension=0, tiled=False)
    ph_part = apply_weight(
        ph_kernel, "ph", offsets, ph_own, ph_cols, multiplier_g, shift_rows[:, None], False
    )
    ph_grad = lax.psum_scatter(ph_part, "col", scatter_dimension=0, tiled=False)

    back = select(take_hot, ph_grad[:, :rank_part], 0)
    back = lax.all_to_all(back, "row", split_axis=0, concat_axis=0, tiled=True)
    returned = select(send_hot, back, 1)
    grad_density = (
        2.0 * pair_grad[:, :rank_part]
        + 2.0 * scale_rows[:, None] * density_factor.astype(jnp.float32)
        + 2.0 * returned
    )
    grad_hole = 2.0 * pair_grad[:, rank_part:]
    grad_ph = 2.0 * ph_grad[:, rank_part:]
    return (grad_density, grad_hole, grad_ph)


def solution(mesh):
    return jax.shard_map(
        local,
        mesh=mesh,
        in_specs=(
            P("row", "col"),
            P("row", "col"),
            P("row", "col"),
            P("row", "col"),
            P("row", "col"),
            P("row", "col"),
            P(),
            P(),
        ),
        out_specs=(P("row", "col"), P("row", "col"), P("row", "col")),
        check_vma=False,
    )
```

```python
import functools

import jax
import jax.numpy as jnp
from jax import lax
from jax.experimental import pallas as pl
from jax.experimental.pallas import tpu as pltpu
from jax.sharding import PartitionSpec as P

shift_value = 2.0
penalty = 2.5


def tile_weight(offset_ref, own_ref, cols_ref, mult_ref, shift):
    parts, block, _ = own_ref.shape
    tile = cols_ref.shape[1]
    gram = None
    for part in range(parts):
        term = lax.dot_general(
            own_ref[part],
            cols_ref[part],
            (((1,), (1,)), ((), ())),
            preferred_element_type=jnp.float32,
        )
        gram = term if gram is None else gram + term
    rows = lax.broadcasted_iota(jnp.int32, (block, tile), 0) + offset_ref[0]
    cols = lax.broadcasted_iota(jnp.int32, (block, tile), 1) + pl.program_id(0) * tile
    resid = jnp.where(rows == cols, shift, 0.0) - gram
    return (mult_ref[...].astype(jnp.float32) + penalty * resid).astype(jnp.bfloat16)


def pair_kernel(offset_ref, own_ref, cols_ref, mult_ref, ham_ref, out_ref):
    @pl.when(pl.program_id(0) == 0)
    def _():
        out_ref[...] = jnp.zeros_like(out_ref)

    half = own_ref.shape[2] // 2
    weight = tile_weight(offset_ref, own_ref, cols_ref, mult_ref, shift_value)
    for part in range(own_ref.shape[0]):
        first = cols_ref[part, :, :half]
        out_ref[part, :, :half] += jnp.dot(
            ham_ref[...], first, preferred_element_type=jnp.float32
        ) - jnp.dot(weight, first, preferred_element_type=jnp.float32)
        out_ref[part, :, half:] -= jnp.dot(
            weight, cols_ref[part, :, half:], preferred_element_type=jnp.float32
        )


def ph_kernel(offset_ref, own_ref, cols_ref, mult_ref, shift_ref, out_ref):
    @pl.when(pl.program_id(0) == 0)
    def _():
        out_ref[...] = jnp.zeros_like(out_ref)

    weight = tile_weight(offset_ref, own_ref, cols_ref, mult_ref, shift_ref[...])
    for part in range(own_ref.shape[0]):
        out_ref[part] -= jnp.dot(weight, cols_ref[part], preferred_element_type=jnp.float32)


def apply_weight(kernel, name, offset, own, cols, mult, extra, extra_tiled):
    parts, block, depth = own.shape
    width = cols.shape[1]
    tile = 512 if width % 512 == 0 else 256
    if extra_tiled:
        extra_spec = pl.BlockSpec((block, tile), lambda j, o: (0, j))
    else:
        extra_spec = pl.BlockSpec(extra.shape, lambda j, o: (0, 0))
    return pl.pallas_call(
        kernel,
        name=name,
        out_shape=jax.ShapeDtypeStruct((parts, block, depth), jnp.float32),
        grid_spec=pltpu.PrefetchScalarGridSpec(
            num_scalar_prefetch=1,
            grid=(width // tile,),
            in_specs=[
                pl.BlockSpec((parts, block, depth), lambda j, o: (0, 0, 0)),
                pl.BlockSpec((parts, tile, depth), lambda j, o: (0, j, 0)),
                pl.BlockSpec((block, tile), lambda j, o: (0, j)),
                extra_spec,
            ],
            out_specs=pl.BlockSpec((parts, block, depth), lambda j, o: (0, 0, 0)),
        ),
        compiler_params=pltpu.CompilerParams(
            dimension_semantics=("arbitrary",), vmem_limit_bytes=40 << 20
        ),
        cost_estimate=pl.CostEstimate(
            flops=(5 if extra_tiled else 4) * block * width * parts * depth,
            bytes_accessed=2 * width * (parts * depth + 2 * block),
            transcendentals=0,
        ),
    )(offset, own, cols, mult, extra)


MESH = pl.DeviceIdType.MESH


def spread_kernel(
    groups,
    col_groups,
    pair_ref,
    ph_ref,
    pair_cols,
    ph_cols,
    pair_own,
    ph_own,
    place_send,
    place_recv,
    own_send,
    own_recv,
    ring_send,
    ring_recv,
    mate_send,
    mate_recv,
    here_sem,
):
    row = lax.axis_index("row")
    col = lax.axis_index("col")
    per = groups // col_groups
    chips = groups // 2
    half = chips // 2
    block = pair_ref.shape[0]
    core = row % 2
    chip = row // 2
    pos = jnp.where(chip % 2 == 0, chip // 2, chips - 1 - chip // 2)

    def row_at(place, which):
        place = (place + chips) % chips
        return jnp.where(place < half, 2 * place, 2 * (chips - 1 - place) + 1) * 2 + which

    ring_to = [(row_at(pos + 1, core), col), (row_at(pos - 1, core), col)]
    mate = (row + 1 - 2 * core, col)
    home = row // per
    moved = col != home
    partner = (col * per + row % per, home)
    peers = [(row, (col + d) % col_groups) for d in range(1, col_groups)]

    barrier = pltpu.get_barrier_semaphore()
    for device in ring_to + [mate] + peers:
        pl.semaphore_signal(barrier, inc=1, device_id=device, device_id_type=MESH)

    @pl.when(moved)
    def _():
        pl.semaphore_signal(barrier, inc=1, device_id=partner, device_id_type=MESH)

    pl.semaphore_wait(barrier, jnp.where(moved, 4 + len(peers), 3 + len(peers)))

    locals_ = [pair_ref, ph_ref]
    cols_ = [pair_cols, ph_cols]
    owns_ = [pair_own, ph_own]

    def placing(a):
        return pltpu.make_async_remote_copy(
            src_ref=locals_[a],
            dst_ref=cols_[a].at[partner[0]],
            send_sem=place_send.at[a],
            recv_sem=place_recv.at[a],
            device_id=partner,
            device_id_type=MESH,
        )

    def staying(a):
        return pltpu.make_async_copy(locals_[a], cols_[a].at[row], here_sem.at[a, 0])

    def keeping(a):
        return pltpu.make_async_copy(locals_[a], owns_[a].at[col], here_sem.at[a, 1])

    def owning(a, d, origin):
        return pltpu.make_async_remote_copy(
            src_ref=locals_[a],
            dst_ref=owns_[a].at[origin],
            send_sem=own_send.at[a, d - 1],
            recv_sem=own_recv.at[a, d - 1],
            device_id=peers[d - 1],
            device_id_type=MESH,
        )

    def piece(a, slot, way, step):
        if step == half:
            return cols_[a].at[slot, pl.ds(way * (block // 2), block // 2)]
        return cols_[a].at[slot]

    def ring(a, way, step, travelled):
        sign = -1 if way == 0 else 1
        ref = piece(a, row_at(pos + sign * travelled, core), way, step)
        return pltpu.make_async_remote_copy(
            src_ref=ref,
            dst_ref=ref,
            send_sem=ring_send.at[a, way, step - 1],
            recv_sem=ring_recv.at[a, way, step - 1],
            device_id=ring_to[way],
            device_id_type=MESH,
        )

    def mating(a, way, step, which):
        sign = -1 if way == 0 else 1
        ref = piece(a, row_at(pos + sign * step, which), way, step)
        return pltpu.make_async_remote_copy(
            src_ref=ref,
            dst_ref=ref,
            send_sem=mate_send.at[a, way, step],
            recv_sem=mate_recv.at[a, way, step],
            device_id=mate,
            device_id_type=MESH,
        )

    for a in range(2):

        @pl.when(moved)
        def _():
            placing(a).start()

        @pl.when(jnp.logical_not(moved))
        def _():
            staying(a).start()

        keeping(a).start()

    for a in range(2):

        @pl.when(moved)
        def _():
            placing(a).wait_recv()

        @pl.when(jnp.logical_not(moved))
        def _():
            staying(a).wait()

        for way in range(2):
            ring(a, way, 1, 0).start()
        mating(a, 0, 0, core).start()

    for a in range(2):
        for d in range(1, col_groups):
            owning(a, d, col).start()

    for step in range(1, half + 1):
        for a in range(2):
            for way in range(2):
                ring(a, way, step, step).wait_recv()
                if step < half:
                    ring(a, way, step + 1, step).start()
                mating(a, way, step, core).start()

    for a in range(2):
        mating(a, 0, 0, 1 - core).wait_recv()
        mating(a, 0, 0, core).wait_send()
        for step in range(1, half + 1):
            for way in range(2):
                mating(a, way, step, 1 - core).wait_recv()
                mating(a, way, step, core).wait_send()
                ring(a, way, step, step - 1).wait_send()
        for d in range(1, col_groups):
            owning(a, d, (col + col_groups - d) % col_groups).wait_recv()
            owning(a, d, col).wait_send()
        keeping(a).wait()

        @pl.when(moved)
        def _():
            placing(a).wait_send()


def spread(groups, col_groups, pair_local, ph_local):
    block, depth = pair_local.shape
    half = groups // 4
    dma = pltpu.SemaphoreType.DMA
    cols = jax.ShapeDtypeStruct((groups, block, depth), pair_local.dtype)
    own = jax.ShapeDtypeStruct((col_groups, block, depth), pair_local.dtype)
    return pl.pallas_call(
        functools.partial(spread_kernel, groups, col_groups),
        name="spread",
        out_shape=(cols, cols, own, own),
        in_specs=[pl.BlockSpec(memory_space=pltpu.VMEM)] * 2,
        out_specs=(pl.BlockSpec(memory_space=pl.ANY),) * 4,
        scratch_shapes=[
            dma((2,)),
            dma((2,)),
            dma((2, max(col_groups - 1, 1))),
            dma((2, max(col_groups - 1, 1))),
            dma((2, 2, half)),
            dma((2, 2, half)),
            dma((2, 2, half + 1)),
            dma((2, 2, half + 1)),
            dma((2, 2)),
        ],
        compiler_params=pltpu.CompilerParams(collective_id=0, has_side_effects=True),
    )(pair_local, ph_local)


def select(one_hot, values, left_axis):
    if values.dtype == jnp.float32:
        precision = lax.Precision.HIGHEST
    else:
        precision = None
    return lax.dot_general(
        one_hot.astype(values.dtype),
        values,
        (((left_axis,), (0,)), ((), ())),
        precision=precision,
        preferred_element_type=jnp.float32,
    ).astype(values.dtype)


def local(
    density_factor,
    hole_factor,
    ph_factor,
    hamiltonian,
    multiplier_q,
    multiplier_g,
    ph_perm,
    block_lengths,
):
    groups = lax.axis_size("row")
    col_groups = lax.axis_size("col")
    row_index = lax.axis_index("row")
    col_index = lax.axis_index("col")
    block, rank_part = density_factor.shape
    width = multiplier_q.shape[1]
    sends = block // groups
    both = ("row", "col")
    pair_local = jnp.concatenate([density_factor, hole_factor], axis=1)

    index = jnp.arange(block, dtype=jnp.int32)
    row_ids = row_index * block + index
    mine = lax.dynamic_slice_in_dim(ph_perm, row_index * block, block)
    source = mine // block
    same_source = (source[:, None] == source[None, :]) & (index[None, :] < index[:, None])
    slot = source * sends + jnp.sum(same_source.astype(jnp.int32), axis=1)
    everywhere = jnp.arange(groups * block, dtype=jnp.int32)
    inverse = jnp.sum(
        jnp.where(ph_perm[None, :] == row_ids[:, None], everywhere[None, :], 0), axis=1
    )
    target = inverse // block
    same_target = (target[:, None] == target[None, :]) & (inverse[None, :] < inverse[:, None])
    outlet = target * sends + jnp.sum(same_target.astype(jnp.int32), axis=1)
    send_hot = outlet[:, None] == index[None, :]
    take_hot = slot[:, None] == index[None, :]

    outgoing = select(send_hot, density_factor, 0)
    incoming = lax.all_to_all(outgoing, "row", split_axis=0, concat_axis=0, tiled=True)
    density_ph = select(take_hot, incoming, 1)
    ph_local = jnp.concatenate([density_ph, ph_factor], axis=1)

    lengths = block_lengths.astype(jnp.float32)
    count = block_lengths.shape[0]
    upto = jnp.arange(count, dtype=jnp.int32)
    ends = jnp.sum(jnp.where(upto[None, :] <= upto[:, None], block_lengths[None, :], 0), axis=1)
    starts = ends - block_lengths

    def member_of(ids):
        inside = (ids[:, None] >= starts[None, :]) & (ids[:, None] < ends[None, :])
        return inside.astype(jnp.float32)

    member = member_of(row_ids)
    member_ph = member_of(mine)
    density_sq = jnp.sum(jnp.square(density_factor.astype(jnp.float32)), axis=1)
    ph_sq = jnp.sum(jnp.square(ph_factor.astype(jnp.float32)), axis=1)
    offset = row_index * block - col_index * width
    holds = (offset >= 0) & (offset < width)
    square = lax.dynamic_slice_in_dim(
        multiplier_g, jnp.clip(offset, 0, width - block), block, axis=1
    )
    keep = (index[:, None] == index[None, :]) & holds
    mult_diag = jnp.sum(jnp.where(keep, square.astype(jnp.float32), 0.0), axis=1)
    sums = lax.psum(
        jnp.stack(
            [
                jnp.sum(member * density_sq[:, None], axis=0),
                jnp.sum(member_ph * (mult_diag - penalty * ph_sq)[:, None], axis=0),
            ]
        ),
        both,
    )
    shift_means = 2.0 * sums[0] / lengths
    scale_means = 2.0 * (sums[1] + penalty * sums[0]) / lengths
    shift_rows = jnp.sum(member_ph * shift_means[None, :], axis=1)
    scale_rows = jnp.sum(member * scale_means[None, :], axis=1)

    pair_cols, ph_cols, pair_own, ph_own = spread(groups, col_groups, pair_local, ph_local)
    pair_cols = pair_cols.reshape(col_groups, width, 2 * rank_part)
    ph_cols = ph_cols.reshape(col_groups, width, 2 * rank_part)
    offsets = offset.reshape(1)
    pair_part = apply_weight(
        pair_kernel, "pair", offsets, pair_own, pair_cols, multiplier_q, hamiltonian, True
    )
    pair_grad = lax.psum_scatter(pair_part, "col", scatter_dimension=0, tiled=False)
    ph_part = apply_weight(
        ph_kernel, "ph", offsets, ph_own, ph_cols, multiplier_g, shift_rows[:, None], False
    )
    ph_grad = lax.psum_scatter(ph_part, "col", scatter_dimension=0, tiled=False)

    back = select(take_hot, ph_grad[:, :rank_part], 0)
    back = lax.all_to_all(back, "row", split_axis=0, concat_axis=0, tiled=True)
    returned = select(send_hot, back, 1)
    grad_density = (
        2.0 * pair_grad[:, :rank_part]
        + 2.0 * scale_rows[:, None] * density_factor.astype(jnp.float32)
        + 2.0 * returned
    )
    grad_hole = 2.0 * pair_grad[:, rank_part:]
    grad_ph = 2.0 * ph_grad[:, rank_part:]
    return (grad_density, grad_hole, grad_ph)


def solution(mesh):
    return jax.shard_map(
        local,
        mesh=mesh,
        in_specs=(
            P("row", "col"),
            P("row", "col"),
            P("row", "col"),
            P("row", "col"),
            P("row", "col"),
            P("row", "col"),
            P(),
            P(),
        ),
        out_specs=(P("row", "col"), P("row", "col"), P("row", "col")),
        check_vma=False,
    )
```

```python
import functools

import jax
import jax.numpy as jnp
from jax import lax
from jax.experimental import pallas as pl
from jax.experimental.pallas import tpu as pltpu
from jax.sharding import PartitionSpec as P

shift_value = 2.0
penalty = 2.5


def tile_weight(offset_ref, own_ref, cols_ref, mult_ref, shift):
    parts, block, _ = own_ref.shape
    tile = cols_ref.shape[1]
    gram = None
    for part in range(parts):
        term = lax.dot_general(
            own_ref[part],
            cols_ref[part],
            (((1,), (1,)), ((), ())),
            preferred_element_type=jnp.float32,
        )
        gram = term if gram is None else gram + term
    rows = lax.broadcasted_iota(jnp.int32, (block, tile), 0) + offset_ref[0]
    cols = lax.broadcasted_iota(jnp.int32, (block, tile), 1) + pl.program_id(0) * tile
    resid = jnp.where(rows == cols, shift, 0.0) - gram
    return (mult_ref[...].astype(jnp.float32) + penalty * resid).astype(jnp.bfloat16)


def pair_kernel(offset_ref, own_ref, cols_ref, mult_ref, ham_ref, out_ref):
    @pl.when(pl.program_id(0) == 0)
    def _():
        out_ref[...] = jnp.zeros_like(out_ref)

    half = own_ref.shape[2] // 2
    weight = tile_weight(offset_ref, own_ref, cols_ref, mult_ref, shift_value)
    for part in range(own_ref.shape[0]):
        first = cols_ref[part, :, :half]
        out_ref[part, :, :half] += jnp.dot(
            ham_ref[...], first, preferred_element_type=jnp.float32
        ) - jnp.dot(weight, first, preferred_element_type=jnp.float32)
        out_ref[part, :, half:] -= jnp.dot(
            weight, cols_ref[part, :, half:], preferred_element_type=jnp.float32
        )


def ph_kernel(offset_ref, own_ref, cols_ref, mult_ref, shift_ref, out_ref):
    @pl.when(pl.program_id(0) == 0)
    def _():
        out_ref[...] = jnp.zeros_like(out_ref)

    weight = tile_weight(offset_ref, own_ref, cols_ref, mult_ref, shift_ref[...])
    for part in range(own_ref.shape[0]):
        out_ref[part] -= jnp.dot(weight, cols_ref[part], preferred_element_type=jnp.float32)


def apply_weight(kernel, name, offset, own, cols, mult, extra, extra_tiled):
    parts, block, depth = own.shape
    width = cols.shape[1]
    tile = 512 if width % 512 == 0 else 256
    if extra_tiled:
        extra_spec = pl.BlockSpec((block, tile), lambda j, o: (0, j))
    else:
        extra_spec = pl.BlockSpec(extra.shape, lambda j, o: (0, 0))
    return pl.pallas_call(
        kernel,
        name=name,
        out_shape=jax.ShapeDtypeStruct((parts, block, depth), jnp.float32),
        grid_spec=pltpu.PrefetchScalarGridSpec(
            num_scalar_prefetch=1,
            grid=(width // tile,),
            in_specs=[
                pl.BlockSpec((parts, block, depth), lambda j, o: (0, 0, 0)),
                pl.BlockSpec((parts, tile, depth), lambda j, o: (0, j, 0)),
                pl.BlockSpec((block, tile), lambda j, o: (0, j)),
                extra_spec,
            ],
            out_specs=pl.BlockSpec((parts, block, depth), lambda j, o: (0, 0, 0)),
        ),
        compiler_params=pltpu.CompilerParams(
            dimension_semantics=("arbitrary",), vmem_limit_bytes=40 << 20
        ),
        cost_estimate=pl.CostEstimate(
            flops=(5 if extra_tiled else 4) * block * width * parts * depth,
            bytes_accessed=2 * width * (parts * depth + 2 * block),
            transcendentals=0,
        ),
    )(offset, own, cols, mult, extra)


MESH = pl.DeviceIdType.MESH


def spread_kernel(
    groups,
    col_groups,
    pair_ref,
    ph_ref,
    stats_ref,
    pair_cols,
    ph_cols,
    pair_own,
    ph_own,
    stats_all,
    place_send,
    place_recv,
    own_send,
    own_recv,
    ring_send,
    ring_recv,
    mate_send,
    mate_recv,
    here_sem,
    stats_send,
    stats_recv,
    rows_send,
    rows_recv,
):
    row = lax.axis_index("row")
    col = lax.axis_index("col")
    per = groups // col_groups
    chips = groups // 2
    half = chips // 2
    block = pair_ref.shape[0]
    core = row % 2
    chip = row // 2
    pos = jnp.where(chip % 2 == 0, chip // 2, chips - 1 - chip // 2)

    def row_at(place, which):
        place = (place + chips) % chips
        return jnp.where(place < half, 2 * place, 2 * (chips - 1 - place) + 1) * 2 + which

    ring_to = [(row_at(pos + 1, core), col), (row_at(pos - 1, core), col)]
    mate = (row + 1 - 2 * core, col)
    home = row // per
    moved = col != home
    partner = (col * per + row % per, home)
    peers = [(row, (col + d) % col_groups) for d in range(1, col_groups)]

    others = [(row + d) % groups for d in range(1, groups)]

    barrier = pltpu.get_barrier_semaphore()
    for device in [(other, col) for other in others] + peers:
        pl.semaphore_signal(barrier, inc=1, device_id=device, device_id_type=MESH)

    @pl.when(moved)
    def _():
        pl.semaphore_signal(barrier, inc=1, device_id=partner, device_id_type=MESH)

    greeted = len(others) + len(peers)
    pl.semaphore_wait(barrier, jnp.where(moved, greeted + 1, greeted))

    locals_ = [pair_ref, ph_ref]
    cols_ = [pair_cols, ph_cols]
    owns_ = [pair_own, ph_own]

    def placing(a):
        return pltpu.make_async_remote_copy(
            src_ref=locals_[a],
            dst_ref=cols_[a].at[partner[0]],
            send_sem=place_send.at[a],
            recv_sem=place_recv.at[a],
            device_id=partner,
            device_id_type=MESH,
        )

    def staying(a):
        return pltpu.make_async_copy(locals_[a], cols_[a].at[row], here_sem.at[a, 0])

    def keeping(a):
        return pltpu.make_async_copy(locals_[a], owns_[a].at[col], here_sem.at[a, 1])

    def owning(a, d, origin):
        return pltpu.make_async_remote_copy(
            src_ref=locals_[a],
            dst_ref=owns_[a].at[origin],
            send_sem=own_send.at[a, d - 1],
            recv_sem=own_recv.at[a, d - 1],
            device_id=peers[d - 1],
            device_id_type=MESH,
        )

    def piece(a, slot, way, step):
        if step == half:
            return cols_[a].at[slot, pl.ds(way * (block // 2), block // 2)]
        return cols_[a].at[slot]

    def ring(a, way, step, travelled):
        sign = -1 if way == 0 else 1
        ref = piece(a, row_at(pos + sign * travelled, core), way, step)
        return pltpu.make_async_remote_copy(
            src_ref=ref,
            dst_ref=ref,
            send_sem=ring_send.at[a, way, step - 1],
            recv_sem=ring_recv.at[a, way, step - 1],
            device_id=ring_to[way],
            device_id_type=MESH,
        )

    def mating(a, way, step, which):
        sign = -1 if way == 0 else 1
        ref = piece(a, row_at(pos + sign * step, which), way, step)
        return pltpu.make_async_remote_copy(
            src_ref=ref,
            dst_ref=ref,
            send_sem=mate_send.at[a, way, step],
            recv_sem=mate_recv.at[a, way, step],
            device_id=mate,
            device_id_type=MESH,
        )

    def stats_here():
        return pltpu.make_async_copy(stats_ref, stats_all.at[row, col], here_sem.at[0, 2])

    def stats_over(d, origin):
        return pltpu.make_async_remote_copy(
            src_ref=stats_ref,
            dst_ref=stats_all.at[row, origin],
            send_sem=stats_send.at[d - 1],
            recv_sem=stats_recv.at[d - 1],
            device_id=peers[d - 1],
            device_id_type=MESH,
        )

    def stats_rows(d, origin):
        return pltpu.make_async_remote_copy(
            src_ref=stats_all.at[origin],
            dst_ref=stats_all.at[origin],
            send_sem=rows_send.at[d - 1],
            recv_sem=rows_recv.at[d - 1],
            device_id=(others[d - 1], col),
            device_id_type=MESH,
        )

    stats_here().start()
    for d in range(1, col_groups):
        stats_over(d, col).start()
    for a in range(2):

        @pl.when(moved)
        def _():
            placing(a).start()

        @pl.when(jnp.logical_not(moved))
        def _():
            staying(a).start()

        keeping(a).start()

    stats_here().wait()
    for d in range(1, col_groups):
        stats_over(d, (col + col_groups - d) % col_groups).wait_recv()
    for d in range(1, groups):
        stats_rows(d, row).start()

    for a in range(2):

        @pl.when(moved)
        def _():
            placing(a).wait_recv()

        @pl.when(jnp.logical_not(moved))
        def _():
            staying(a).wait()

        for way in range(2):
            ring(a, way, 1, 0).start()
        mating(a, 0, 0, core).start()

    for a in range(2):
        for d in range(1, col_groups):
            owning(a, d, col).start()

    for step in range(1, half + 1):
        for a in range(2):
            for way in range(2):
                ring(a, way, step, step).wait_recv()
                if step < half:
                    ring(a, way, step + 1, step).start()
                mating(a, way, step, core).start()

    for d in range(1, col_groups):
        stats_over(d, col).wait_send()
    for d in range(1, groups):
        stats_rows(d, (row + groups - d) % groups).wait_recv()
        stats_rows(d, row).wait_send()
    for a in range(2):
        mating(a, 0, 0, 1 - core).wait_recv()
        mating(a, 0, 0, core).wait_send()
        for step in range(1, half + 1):
            for way in range(2):
                mating(a, way, step, 1 - core).wait_recv()
                mating(a, way, step, core).wait_send()
                ring(a, way, step, step - 1).wait_send()
        for d in range(1, col_groups):
            owning(a, d, (col + col_groups - d) % col_groups).wait_recv()
            owning(a, d, col).wait_send()
        keeping(a).wait()

        @pl.when(moved)
        def _():
            placing(a).wait_send()


def spread(groups, col_groups, pair_local, ph_local, stats):
    block, depth = pair_local.shape
    half = groups // 4
    dma = pltpu.SemaphoreType.DMA
    cols = jax.ShapeDtypeStruct((groups, block, depth), pair_local.dtype)
    own = jax.ShapeDtypeStruct((col_groups, block, depth), pair_local.dtype)
    return pl.pallas_call(
        functools.partial(spread_kernel, groups, col_groups),
        name="spread",
        out_shape=(
            cols,
            cols,
            own,
            own,
            jax.ShapeDtypeStruct((groups, col_groups) + stats.shape, stats.dtype),
        ),
        in_specs=[pl.BlockSpec(memory_space=pltpu.VMEM)] * 3,
        out_specs=(pl.BlockSpec(memory_space=pl.ANY),) * 5,
        scratch_shapes=[
            dma((2,)),
            dma((2,)),
            dma((2, max(col_groups - 1, 1))),
            dma((2, max(col_groups - 1, 1))),
            dma((2, 2, half)),
            dma((2, 2, half)),
            dma((2, 2, half + 1)),
            dma((2, 2, half + 1)),
            dma((2, 3)),
            dma((max(col_groups - 1, 1),)),
            dma((max(col_groups - 1, 1),)),
            dma((groups - 1,)),
            dma((groups - 1,)),
        ],
        compiler_params=pltpu.CompilerParams(collective_id=0, has_side_effects=True),
    )(pair_local, ph_local, stats)


def select(one_hot, values, left_axis):
    if values.dtype == jnp.float32:
        precision = lax.Precision.HIGHEST
    else:
        precision = None
    return lax.dot_general(
        one_hot.astype(values.dtype),
        values,
        (((left_axis,), (0,)), ((), ())),
        precision=precision,
        preferred_element_type=jnp.float32,
    ).astype(values.dtype)


def local(
    density_factor,
    hole_factor,
    ph_factor,
    hamiltonian,
    multiplier_q,
    multiplier_g,
    ph_perm,
    block_lengths,
):
    groups = lax.axis_size("row")
    col_groups = lax.axis_size("col")
    row_index = lax.axis_index("row")
    col_index = lax.axis_index("col")
    block, rank_part = density_factor.shape
    width = multiplier_q.shape[1]
    sends = block // groups
    pair_local = jnp.concatenate([density_factor, hole_factor], axis=1)

    index = jnp.arange(block, dtype=jnp.int32)
    row_ids = row_index * block + index
    mine = lax.dynamic_slice_in_dim(ph_perm, row_index * block, block)
    source = mine // block
    same_source = (source[:, None] == source[None, :]) & (index[None, :] < index[:, None])
    slot = source * sends + jnp.sum(same_source.astype(jnp.int32), axis=1)
    everywhere = jnp.arange(groups * block, dtype=jnp.int32)
    inverse = jnp.sum(
        jnp.where(ph_perm[None, :] == row_ids[:, None], everywhere[None, :], 0), axis=1
    )
    target = inverse // block
    same_target = (target[:, None] == target[None, :]) & (inverse[None, :] < inverse[:, None])
    outlet = target * sends + jnp.sum(same_target.astype(jnp.int32), axis=1)
    send_hot = outlet[:, None] == index[None, :]
    take_hot = slot[:, None] == index[None, :]

    outgoing = select(send_hot, density_factor, 0)
    incoming = lax.all_to_all(outgoing, "row", split_axis=0, concat_axis=0, tiled=True)
    density_ph = select(take_hot, incoming, 1)
    ph_local = jnp.concatenate([density_ph, ph_factor], axis=1)

    lengths = block_lengths.astype(jnp.float32)
    count = block_lengths.shape[0]
    upto = jnp.arange(count, dtype=jnp.int32)
    ends = jnp.sum(jnp.where(upto[None, :] <= upto[:, None], block_lengths[None, :], 0), axis=1)
    starts = ends - block_lengths

    def member_of(ids):
        inside = (ids[:, None] >= starts[None, :]) & (ids[:, None] < ends[None, :])
        return inside.astype(jnp.float32)

    member = member_of(row_ids)
    member_ph = member_of(mine)
    density_sq = jnp.sum(jnp.square(density_factor.astype(jnp.float32)), axis=1)
    ph_sq = jnp.sum(jnp.square(ph_factor.astype(jnp.float32)), axis=1)
    offset = row_index * block - col_index * width
    holds = (offset >= 0) & (offset < width)
    square = lax.dynamic_slice_in_dim(
        multiplier_g, jnp.clip(offset, 0, width - block), block, axis=1
    )
    keep = (index[:, None] == index[None, :]) & holds
    mult_diag = jnp.sum(jnp.where(keep, square.astype(jnp.float32), 0.0), axis=1)
    sums = jnp.stack(
        [
            jnp.sum(member * density_sq[:, None], axis=0),
            jnp.sum(member_ph * (mult_diag - penalty * ph_sq)[:, None], axis=0),
        ]
    )
    stats = jnp.pad(sums, ((0, 6), (0, -count % 128)))
    pair_cols, ph_cols, pair_own, ph_own, stats_all = spread(
        groups, col_groups, pair_local, ph_local, stats
    )
    sums = jnp.sum(stats_all, axis=(0, 1))[:, :count]
    shift_means = 2.0 * sums[0] / lengths
    scale_means = 2.0 * (sums[1] + penalty * sums[0]) / lengths
    shift_rows = jnp.sum(member_ph * shift_means[None, :], axis=1)
    scale_rows = jnp.sum(member * scale_means[None, :], axis=1)

    pair_cols = pair_cols.reshape(col_groups, width, 2 * rank_part)
    ph_cols = ph_cols.reshape(col_groups, width, 2 * rank_part)
    offsets = offset.reshape(1)
    pair_part = apply_weight(
        pair_kernel, "pair", offsets, pair_own, pair_cols, multiplier_q, hamiltonian, True
    )
    pair_grad = lax.psum_scatter(pair_part, "col", scatter_dimension=0, tiled=False)
    ph_part = apply_weight(
        ph_kernel, "ph", offsets, ph_own, ph_cols, multiplier_g, shift_rows[:, None], False
    )
    ph_grad = lax.psum_scatter(ph_part, "col", scatter_dimension=0, tiled=False)

    back = select(take_hot, ph_grad[:, :rank_part], 0)
    back = lax.all_to_all(back, "row", split_axis=0, concat_axis=0, tiled=True)
    returned = select(send_hot, back, 1)
    grad_density = (
        2.0 * pair_grad[:, :rank_part]
        + 2.0 * scale_rows[:, None] * density_factor.astype(jnp.float32)
        + 2.0 * returned
    )
    grad_hole = 2.0 * pair_grad[:, rank_part:]
    grad_ph = 2.0 * ph_grad[:, rank_part:]
    return (grad_density, grad_hole, grad_ph)


def solution(mesh):
    return jax.shard_map(
        local,
        mesh=mesh,
        in_specs=(
            P("row", "col"),
            P("row", "col"),
            P("row", "col"),
            P("row", "col"),
            P("row", "col"),
            P("row", "col"),
            P(),
            P(),
        ),
        out_specs=(P("row", "col"), P("row", "col"), P("row", "col")),
        check_vma=False,
    )
```

```python
import functools

import jax
import jax.numpy as jnp
from jax import lax
from jax.experimental import pallas as pl
from jax.experimental.pallas import tpu as pltpu
from jax.sharding import PartitionSpec as P

shift_value = 2.0
penalty = 2.5


MESH = pl.DeviceIdType.MESH


def spread_kernel(
    groups,
    col_groups,
    pair_ref,
    ph_ref,
    stats_ref,
    member_ref,
    lengths_ref,
    ham_hbm,
    mult_q_hbm,
    mult_g_hbm,
    pair_out,
    ph_out,
    sums_out,
    pair_cols,
    ph_cols,
    pair_own,
    ph_own,
    stats_all,
    ham,
    mult_q,
    mult_g,
    pair_acc,
    ph_acc,
    pair_in,
    ph_in,
    place_send,
    place_recv,
    own_send,
    own_recv,
    ring_send,
    ring_recv,
    mate_send,
    mate_recv,
    here_sem,
    stats_send,
    stats_recv,
    rows_send,
    rows_recv,
    fetch_sem,
    swap_send,
    swap_recv,
):
    row = lax.axis_index("row")
    col = lax.axis_index("col")
    per = groups // col_groups
    chips = groups // 2
    half = chips // 2
    block = pair_ref.shape[0]
    core = row % 2
    chip = row // 2
    pos = jnp.where(chip % 2 == 0, chip // 2, chips - 1 - chip // 2)

    def row_at(place, which):
        place = (place + chips) % chips
        return jnp.where(place < half, 2 * place, 2 * (chips - 1 - place) + 1) * 2 + which

    ring_to = [(row_at(pos + 1, core), col), (row_at(pos - 1, core), col)]
    mate = (row + 1 - 2 * core, col)
    home = row // per
    moved = col != home
    partner = (col * per + row % per, home)
    peers = [(row, (col + d) % col_groups) for d in range(1, col_groups)]

    others = [(row + d) % groups for d in range(1, groups)]

    barrier = pltpu.get_barrier_semaphore()
    for device in [(other, col) for other in others] + peers:
        pl.semaphore_signal(barrier, inc=1, device_id=device, device_id_type=MESH)

    @pl.when(moved)
    def _():
        pl.semaphore_signal(barrier, inc=1, device_id=partner, device_id_type=MESH)

    greeted = len(others) + len(peers)
    pl.semaphore_wait(barrier, jnp.where(moved, greeted + 1, greeted))

    locals_ = [pair_ref, ph_ref]
    cols_ = [pair_cols, ph_cols]
    owns_ = [pair_own, ph_own]

    def placing(a):
        return pltpu.make_async_remote_copy(
            src_ref=locals_[a],
            dst_ref=cols_[a].at[partner[0]],
            send_sem=place_send.at[a],
            recv_sem=place_recv.at[a],
            device_id=partner,
            device_id_type=MESH,
        )

    def staying(a):
        return pltpu.make_async_copy(locals_[a], cols_[a].at[row], here_sem.at[a, 0])

    def keeping(a):
        return pltpu.make_async_copy(locals_[a], owns_[a].at[col], here_sem.at[a, 1])

    def owning(a, d, origin):
        return pltpu.make_async_remote_copy(
            src_ref=locals_[a],
            dst_ref=owns_[a].at[origin],
            send_sem=own_send.at[a, d - 1],
            recv_sem=own_recv.at[a, d - 1],
            device_id=peers[d - 1],
            device_id_type=MESH,
        )

    def piece(a, slot, way, step):
        if step == half:
            return cols_[a].at[slot, pl.ds(way * (block // 2), block // 2)]
        return cols_[a].at[slot]

    def ring(a, way, step, travelled):
        sign = -1 if way == 0 else 1
        ref = piece(a, row_at(pos + sign * travelled, core), way, step)
        return pltpu.make_async_remote_copy(
            src_ref=ref,
            dst_ref=ref,
            send_sem=ring_send.at[a, way, step - 1],
            recv_sem=ring_recv.at[a, way, step - 1],
            device_id=ring_to[way],
            device_id_type=MESH,
        )

    def mating(a, way, step, which):
        sign = -1 if way == 0 else 1
        ref = piece(a, row_at(pos + sign * step, which), way, step)
        return pltpu.make_async_remote_copy(
            src_ref=ref,
            dst_ref=ref,
            send_sem=mate_send.at[a, way, step],
            recv_sem=mate_recv.at[a, way, step],
            device_id=mate,
            device_id_type=MESH,
        )

    def stats_here():
        return pltpu.make_async_copy(stats_ref, stats_all.at[row, col], here_sem.at[0, 2])

    def stats_over(d, origin):
        return pltpu.make_async_remote_copy(
            src_ref=stats_ref,
            dst_ref=stats_all.at[row, origin],
            send_sem=stats_send.at[d - 1],
            recv_sem=stats_recv.at[d - 1],
            device_id=peers[d - 1],
            device_id_type=MESH,
        )

    def stats_rows(d, origin):
        return pltpu.make_async_remote_copy(
            src_ref=stats_all.at[origin],
            dst_ref=stats_all.at[origin],
            send_sem=rows_send.at[d - 1],
            recv_sem=rows_recv.at[d - 1],
            device_id=(others[d - 1], col),
            device_id_type=MESH,
        )

    stats_here().start()
    for d in range(1, col_groups):
        stats_over(d, col).start()
    for a in range(2):

        @pl.when(moved)
        def _():
            placing(a).start()

        @pl.when(jnp.logical_not(moved))
        def _():
            staying(a).start()

        keeping(a).start()

    stats_here().wait()
    for d in range(1, col_groups):
        stats_over(d, (col + col_groups - d) % col_groups).wait_recv()
    for d in range(1, groups):
        stats_rows(d, row).start()

    def launch(a):
        @pl.when(moved)
        def _():
            placing(a).wait_recv()

        @pl.when(jnp.logical_not(moved))
        def _():
            staying(a).wait()

        for way in range(2):
            ring(a, way, 1, 0).start()
        mating(a, 0, 0, core).start()
        for d in range(1, col_groups):
            owning(a, d, col).start()

    def arrive(a, step):
        for way in range(2):
            ring(a, way, step, step).wait_recv()
            if step < half:
                ring(a, way, step + 1, step).start()
            mating(a, way, step, core).start()

    def settle(a):
        mating(a, 0, 0, 1 - core).wait_recv()
        for step in range(1, half + 1):
            for way in range(2):
                mating(a, way, step, 1 - core).wait_recv()
        for d in range(1, col_groups):
            owning(a, d, (col + col_groups - d) % col_groups).wait_recv()
        keeping(a).wait()

    def drain(a):
        mating(a, 0, 0, core).wait_send()
        for step in range(1, half + 1):
            for way in range(2):
                mating(a, way, step, core).wait_send()
                ring(a, way, step, step - 1).wait_send()
        for d in range(1, col_groups):
            owning(a, d, col).wait_send()

        @pl.when(moved)
        def _():
            placing(a).wait_send()

    accs_ = [pair_acc, ph_acc]
    ins_ = [pair_in, ph_in]

    def swapping(a, d):
        return pltpu.make_async_remote_copy(
            src_ref=accs_[a].at[(col + d) % col_groups],
            dst_ref=ins_[a].at[d - 1],
            send_sem=swap_send.at[a, d - 1],
            recv_sem=swap_recv.at[a, d - 1],
            device_id=peers[d - 1],
            device_id_type=MESH,
        )

    def finish(a, out):
        total = accs_[a][col]
        for d in range(1, col_groups):
            swapping(a, d).wait_recv()
            total = total + ins_[a][d - 1]
        out[...] = 2.0 * total

    depth = pair_ref.shape[1]
    joined = 2 if per % 2 == 0 else 1
    tile = joined * block
    tiles = per // joined
    offset = row * block - col * per * block

    def weighted(a, t, mult, shift):
        gram = None
        tiles_of = []
        for part in range(col_groups):
            there = cols_[a][pl.ds(part * per + t * joined, joined)].reshape(tile, depth)
            tiles_of.append(there)
            term = lax.dot_general(
                owns_[a][part],
                there,
                (((1,), (1,)), ((), ())),
                preferred_element_type=jnp.float32,
            )
            gram = term if gram is None else gram + term
        rows = lax.broadcasted_iota(jnp.int32, (block, tile), 0) + offset
        places = lax.broadcasted_iota(jnp.int32, (block, tile), 1) + t * tile
        resid = jnp.where(rows == places, shift, 0.0) - gram
        span = pl.ds(pl.multiple_of(t * tile, 128), tile)
        full = mult[:, span].astype(jnp.float32) + penalty * resid
        return full.astype(jnp.bfloat16), tiles_of, span

    def pair_tiles(first, last):
        @pl.loop(first, last)
        def _(t):
            weight, tiles_of, span = weighted(0, t, mult_q, shift_value)
            for part in range(col_groups):
                left = tiles_of[part][:, : depth // 2]
                right = tiles_of[part][:, depth // 2 :]
                pair_acc[part, :, : depth // 2] += jnp.dot(
                    ham[:, span], left, preferred_element_type=jnp.float32
                ) - jnp.dot(weight, left, preferred_element_type=jnp.float32)
                pair_acc[part, :, depth // 2 :] -= jnp.dot(
                    weight, right, preferred_element_type=jnp.float32
                )

    def ph_tiles(shift):
        @pl.loop(0, tiles)
        def _(t):
            weight, tiles_of, _span = weighted(1, t, mult_g, shift)
            for part in range(col_groups):
                ph_acc[part] -= jnp.dot(
                    weight, tiles_of[part], preferred_element_type=jnp.float32
                )

    fetches = [
        pltpu.make_async_copy(mult_q_hbm, mult_q, fetch_sem.at[0]),
        pltpu.make_async_copy(ham_hbm, ham, fetch_sem.at[1]),
        pltpu.make_async_copy(mult_g_hbm, mult_g, fetch_sem.at[2]),
    ]
    lag = min(2, half)

    launch(0)
    for fetch in fetches:
        fetch.start()
    pair_acc[...] = jnp.zeros_like(pair_acc)
    ph_acc[...] = jnp.zeros_like(ph_acc)
    for step in range(1, half + 1):
        arrive(0, step)
        if step == lag:
            launch(1)
        if step > lag:
            arrive(1, step - lag)
    settle(0)
    fetches[0].wait()
    fetches[1].wait()
    for k in range(lag):
        pair_tiles(tiles * k // lag, tiles * (k + 1) // lag)
        arrive(1, half - lag + 1 + k)
    for d in range(1, col_groups):
        swapping(0, d).start()

    for d in range(1, col_groups):
        stats_over(d, col).wait_send()
    for d in range(1, groups):
        stats_rows(d, (row + groups - d) % groups).wait_recv()
        stats_rows(d, row).wait_send()
    sums = jnp.sum(stats_all[...].reshape((groups * col_groups,) + stats_ref.shape), axis=0)
    sums_out[...] = sums
    means = 2.0 * sums[0:1] / lengths_ref[0:1]
    shift = jnp.sum(member_ref[...] * means, axis=1, keepdims=True)

    settle(1)
    fetches[2].wait()
    ph_tiles(shift)
    finish(0, pair_out)
    for d in range(1, col_groups):
        swapping(1, d).start()
    drain(0)
    drain(1)
    finish(1, ph_out)
    for a in range(2):
        for d in range(1, col_groups):
            swapping(a, d).wait_send()


def spread(groups, col_groups, pair_local, ph_local, stats, member, lengths, ham, mult_q, mult_g):
    block, depth = pair_local.shape
    half = groups // 4
    over = max(col_groups - 1, 1)
    dma = pltpu.SemaphoreType.DMA
    kind = pair_local.dtype
    grad = jax.ShapeDtypeStruct((block, depth), jnp.float32)
    vmem = pl.BlockSpec(memory_space=pltpu.VMEM)
    hbm = pl.BlockSpec(memory_space=pl.ANY)
    return pl.pallas_call(
        functools.partial(spread_kernel, groups, col_groups),
        name="spread",
        out_shape=(grad, grad, jax.ShapeDtypeStruct(stats.shape, stats.dtype)),
        in_specs=[vmem] * 5 + [hbm] * 3,
        out_specs=(vmem,) * 3,
        scratch_shapes=[
            pltpu.VMEM((groups, block, depth), kind),
            pltpu.VMEM((groups, block, depth), kind),
            pltpu.VMEM((col_groups, block, depth), kind),
            pltpu.VMEM((col_groups, block, depth), kind),
            pltpu.VMEM((groups, col_groups) + stats.shape, stats.dtype),
            pltpu.VMEM(ham.shape, ham.dtype),
            pltpu.VMEM(mult_q.shape, mult_q.dtype),
            pltpu.VMEM(mult_g.shape, mult_g.dtype),
            pltpu.VMEM((col_groups, block, depth), jnp.float32),
            pltpu.VMEM((col_groups, block, depth), jnp.float32),
            pltpu.VMEM((over, block, depth), jnp.float32),
            pltpu.VMEM((over, block, depth), jnp.float32),
            dma((2,)),
            dma((2,)),
            dma((2, over)),
            dma((2, over)),
            dma((2, 2, half)),
            dma((2, 2, half)),
            dma((2, 2, half + 1)),
            dma((2, 2, half + 1)),
            dma((2, 3)),
            dma((over,)),
            dma((over,)),
            dma((groups - 1,)),
            dma((groups - 1,)),
            dma((3,)),
            dma((2, over)),
            dma((2, over)),
        ],
        compiler_params=pltpu.CompilerParams(
            collective_id=0, has_side_effects=True, vmem_limit_bytes=56 << 20
        ),
    )(pair_local, ph_local, stats, member, lengths, ham, mult_q, mult_g)


def select(one_hot, values, left_axis):
    if values.dtype == jnp.float32:
        precision = lax.Precision.HIGHEST
    else:
        precision = None
    return lax.dot_general(
        one_hot.astype(values.dtype),
        values,
        (((left_axis,), (0,)), ((), ())),
        precision=precision,
        preferred_element_type=jnp.float32,
    ).astype(values.dtype)


def local(
    density_factor,
    hole_factor,
    ph_factor,
    hamiltonian,
    multiplier_q,
    multiplier_g,
    ph_perm,
    block_lengths,
):
    groups = lax.axis_size("row")
    col_groups = lax.axis_size("col")
    row_index = lax.axis_index("row")
    col_index = lax.axis_index("col")
    block, rank_part = density_factor.shape
    width = multiplier_q.shape[1]
    sends = block // groups
    pair_local = jnp.concatenate([density_factor, hole_factor], axis=1)

    index = jnp.arange(block, dtype=jnp.int32)
    row_ids = row_index * block + index
    mine = lax.dynamic_slice_in_dim(ph_perm, row_index * block, block)
    source = mine // block
    same_source = (source[:, None] == source[None, :]) & (index[None, :] < index[:, None])
    slot = source * sends + jnp.sum(same_source.astype(jnp.int32), axis=1)
    everywhere = jnp.arange(groups * block, dtype=jnp.int32)
    inverse = jnp.sum(
        jnp.where(ph_perm[None, :] == row_ids[:, None], everywhere[None, :], 0), axis=1
    )
    target = inverse // block
    same_target = (target[:, None] == target[None, :]) & (inverse[None, :] < inverse[:, None])
    outlet = target * sends + jnp.sum(same_target.astype(jnp.int32), axis=1)
    send_hot = outlet[:, None] == index[None, :]
    take_hot = slot[:, None] == index[None, :]

    outgoing = select(send_hot, density_factor, 0)
    incoming = lax.all_to_all(outgoing, "row", split_axis=0, concat_axis=0, tiled=True)
    density_ph = select(take_hot, incoming, 1)
    ph_local = jnp.concatenate([density_ph, ph_factor], axis=1)

    lengths = block_lengths.astype(jnp.float32)
    count = block_lengths.shape[0]
    upto = jnp.arange(count, dtype=jnp.int32)
    ends = jnp.sum(jnp.where(upto[None, :] <= upto[:, None], block_lengths[None, :], 0), axis=1)
    starts = ends - block_lengths

    def member_of(ids):
        inside = (ids[:, None] >= starts[None, :]) & (ids[:, None] < ends[None, :])
        return inside.astype(jnp.float32)

    member = member_of(row_ids)
    member_ph = member_of(mine)
    density_sq = jnp.sum(jnp.square(density_factor.astype(jnp.float32)), axis=1)
    ph_sq = jnp.sum(jnp.square(ph_factor.astype(jnp.float32)), axis=1)
    offset = row_index * block - col_index * width
    holds = (offset >= 0) & (offset < width)
    square = lax.dynamic_slice_in_dim(
        multiplier_g, jnp.clip(offset, 0, width - block), block, axis=1
    )
    keep = (index[:, None] == index[None, :]) & holds
    mult_diag = jnp.sum(jnp.where(keep, square.astype(jnp.float32), 0.0), axis=1)
    sums = jnp.stack(
        [
            jnp.sum(member * density_sq[:, None], axis=0),
            jnp.sum(member_ph * (mult_diag - penalty * ph_sq)[:, None], axis=0),
        ]
    )
    stats = jnp.pad(sums, ((0, 6), (0, -count % 128)))
    lanes = ((0, 0), (0, -count % 128))
    pair_grad, ph_grad, sums = spread(
        groups,
        col_groups,
        pair_local,
        ph_local,
        stats,
        jnp.pad(member_ph, lanes),
        jnp.pad(jnp.broadcast_to(lengths, (8, count)), lanes, constant_values=1.0),
        hamiltonian,
        multiplier_q,
        multiplier_g,
    )
    sums = sums[:, :count]
    scale_means = 2.0 * (sums[1] + penalty * sums[0]) / lengths
    scale_rows = jnp.sum(member * scale_means[None, :], axis=1)

    back = select(take_hot, ph_grad[:, :rank_part], 0)
    back = lax.all_to_all(back, "row", split_axis=0, concat_axis=0, tiled=True)
    returned = select(send_hot, back, 1)
    grad_density = (
        pair_grad[:, :rank_part]
        + 2.0 * scale_rows[:, None] * density_factor.astype(jnp.float32)
        + returned
    )
    grad_hole = pair_grad[:, rank_part:]
    grad_ph = ph_grad[:, rank_part:]
    return (grad_density, grad_hole, grad_ph)


def solution(mesh):
    return jax.shard_map(
        local,
        mesh=mesh,
        in_specs=(
            P("row", "col"),
            P("row", "col"),
            P("row", "col"),
            P("row", "col"),
            P("row", "col"),
            P("row", "col"),
            P(),
            P(),
        ),
        out_specs=(P("row", "col"), P("row", "col"), P("row", "col")),
        check_vma=False,
    )
```

```python
import functools

import jax
import jax.numpy as jnp
from jax import lax
from jax.experimental import pallas as pl
from jax.experimental.pallas import tpu as pltpu
from jax.sharding import PartitionSpec as P

shift_value = 2.0
penalty = 2.5


MESH = pl.DeviceIdType.MESH


def spread_kernel(
    groups,
    col_groups,
    pair_ref,
    ph_ref,
    stats_ref,
    member_ref,
    lengths_ref,
    ham_hbm,
    mult_q_hbm,
    mult_g_hbm,
    pair_out,
    ph_out,
    sums_out,
    pair_cols,
    ph_cols,
    pair_own,
    ph_own,
    stats_all,
    ham,
    mult_q,
    mult_g,
    pair_acc,
    ph_acc,
    pair_in,
    ph_in,
    place_send,
    place_recv,
    own_send,
    own_recv,
    ring_send,
    ring_recv,
    mate_send,
    mate_recv,
    here_sem,
    stats_send,
    stats_recv,
    rows_send,
    rows_recv,
    fetch_sem,
    swap_send,
    swap_recv,
):
    row = lax.axis_index("row")
    col = lax.axis_index("col")
    per = groups // col_groups
    chips = groups // 2
    half = chips // 2
    block = pair_ref.shape[0]
    core = row % 2
    chip = row // 2
    pos = jnp.where(chip % 2 == 0, chip // 2, chips - 1 - chip // 2)

    def row_at(place, which):
        place = (place + chips) % chips
        return jnp.where(place < half, 2 * place, 2 * (chips - 1 - place) + 1) * 2 + which

    ring_to = [(row_at(pos + 1, core), col), (row_at(pos - 1, core), col)]
    mate = (row + 1 - 2 * core, col)
    home = row // per
    moved = col != home
    partner = (col * per + row % per, home)
    peers = [(row, (col + d) % col_groups) for d in range(1, col_groups)]

    others = [(row + d) % groups for d in range(1, groups)]

    barrier = pltpu.get_barrier_semaphore()
    for device in [(other, col) for other in others] + peers:
        pl.semaphore_signal(barrier, inc=1, device_id=device, device_id_type=MESH)

    @pl.when(moved)
    def _():
        pl.semaphore_signal(barrier, inc=1, device_id=partner, device_id_type=MESH)

    greeted = len(others) + len(peers)
    pl.semaphore_wait(barrier, jnp.where(moved, greeted + 1, greeted))

    locals_ = [pair_ref, ph_ref]
    cols_ = [pair_cols, ph_cols]
    owns_ = [pair_own, ph_own]

    def placing(a):
        return pltpu.make_async_remote_copy(
            src_ref=locals_[a],
            dst_ref=cols_[a].at[partner[0]],
            send_sem=place_send.at[a],
            recv_sem=place_recv.at[a],
            device_id=partner,
            device_id_type=MESH,
        )

    def staying(a):
        return pltpu.make_async_copy(locals_[a], cols_[a].at[row], here_sem.at[a, 0])

    def keeping(a):
        return pltpu.make_async_copy(locals_[a], owns_[a].at[col], here_sem.at[a, 1])

    def owning(a, d, origin):
        return pltpu.make_async_remote_copy(
            src_ref=locals_[a],
            dst_ref=owns_[a].at[origin],
            send_sem=own_send.at[a, d - 1],
            recv_sem=own_recv.at[a, d - 1],
            device_id=peers[d - 1],
            device_id_type=MESH,
        )

    def piece(a, slot, way, step):
        if step == half:
            return cols_[a].at[slot, pl.ds(way * (block // 2), block // 2)]
        return cols_[a].at[slot]

    def ring(a, way, step, travelled):
        sign = -1 if way == 0 else 1
        ref = piece(a, row_at(pos + sign * travelled, core), way, step)
        return pltpu.make_async_remote_copy(
            src_ref=ref,
            dst_ref=ref,
            send_sem=ring_send.at[a, way, step - 1],
            recv_sem=ring_recv.at[a, way, step - 1],
            device_id=ring_to[way],
            device_id_type=MESH,
        )

    def mating(a, way, step, which):
        sign = -1 if way == 0 else 1
        ref = piece(a, row_at(pos + sign * step, which), way, step)
        return pltpu.make_async_remote_copy(
            src_ref=ref,
            dst_ref=ref,
            send_sem=mate_send.at[a, way, step],
            recv_sem=mate_recv.at[a, way, step],
            device_id=mate,
            device_id_type=MESH,
        )

    def stats_here():
        return pltpu.make_async_copy(stats_ref, stats_all.at[row, col], here_sem.at[0, 2])

    def stats_over(d, origin):
        return pltpu.make_async_remote_copy(
            src_ref=stats_ref,
            dst_ref=stats_all.at[row, origin],
            send_sem=stats_send.at[d - 1],
            recv_sem=stats_recv.at[d - 1],
            device_id=peers[d - 1],
            device_id_type=MESH,
        )

    def stats_rows(d, origin):
        return pltpu.make_async_remote_copy(
            src_ref=stats_all.at[origin],
            dst_ref=stats_all.at[origin],
            send_sem=rows_send.at[d - 1],
            recv_sem=rows_recv.at[d - 1],
            device_id=(others[d - 1], col),
            device_id_type=MESH,
        )

    stats_here().start()
    for d in range(1, col_groups):
        stats_over(d, col).start()
    def place(a):
        @pl.when(moved)
        def _():
            placing(a).start()

        @pl.when(jnp.logical_not(moved))
        def _():
            staying(a).start()

        keeping(a).start()

    place(0)

    stats_here().wait()
    for d in range(1, col_groups):
        stats_over(d, (col + col_groups - d) % col_groups).wait_recv()
    for d in range(1, groups):
        stats_rows(d, row).start()

    def launch(a):
        @pl.when(moved)
        def _():
            placing(a).wait_recv()

        @pl.when(jnp.logical_not(moved))
        def _():
            staying(a).wait()

        for way in range(2):
            ring(a, way, 1, 0).start()
        mating(a, 0, 0, core).start()

    def lend(a):
        for d in range(1, col_groups):
            owning(a, d, col).start()

    def arrive(a, step):
        for way in range(2):
            ring(a, way, step, step).wait_recv()
            if step < half:
                ring(a, way, step + 1, step).start()
            mating(a, way, step, core).start()

    def settle(a):
        mating(a, 0, 0, 1 - core).wait_recv()
        for step in range(1, half + 1):
            for way in range(2):
                mating(a, way, step, 1 - core).wait_recv()
        for d in range(1, col_groups):
            owning(a, d, (col + col_groups - d) % col_groups).wait_recv()
        keeping(a).wait()

    def drain(a):
        mating(a, 0, 0, core).wait_send()
        for step in range(1, half + 1):
            for way in range(2):
                mating(a, way, step, core).wait_send()
                ring(a, way, step, step - 1).wait_send()
        for d in range(1, col_groups):
            owning(a, d, col).wait_send()

        @pl.when(moved)
        def _():
            placing(a).wait_send()

    accs_ = [pair_acc, ph_acc]
    ins_ = [pair_in, ph_in]

    every = slice(0, block)
    halves = [slice(0, block // 2), slice(block // 2, block)]

    def swapping(a, d, slot, rows):
        return pltpu.make_async_remote_copy(
            src_ref=accs_[a].at[(col + d) % col_groups, rows],
            dst_ref=ins_[a].at[d - 1, rows],
            send_sem=swap_send.at[slot, d - 1],
            recv_sem=swap_recv.at[slot, d - 1],
            device_id=peers[d - 1],
            device_id_type=MESH,
        )

    def finish(a, out, slot, rows):
        total = accs_[a][col, rows]
        for d in range(1, col_groups):
            swapping(a, d, slot, rows).wait_recv()
            total = total + ins_[a][d - 1, rows]
        out[rows] = 2.0 * total

    depth = pair_ref.shape[1]
    joined = 2 if per % 2 == 0 else 1
    tile = joined * block
    tiles = per // joined
    offset = row * block - col * per * block

    def weighted(a, t, mult, shift, taken):
        gram = None
        tiles_of = []
        for part in range(col_groups):
            there = cols_[a][pl.ds(part * per + t * joined, joined)].reshape(tile, depth)
            tiles_of.append(there)
            term = lax.dot_general(
                owns_[a][part, taken],
                there,
                (((1,), (1,)), ((), ())),
                preferred_element_type=jnp.float32,
            )
            gram = term if gram is None else gram + term
        dims = (taken.stop - taken.start, tile)
        rows = lax.broadcasted_iota(jnp.int32, dims, 0) + (offset + taken.start)
        places = lax.broadcasted_iota(jnp.int32, dims, 1) + t * tile
        resid = jnp.where(rows == places, shift, 0.0) - gram
        span = pl.ds(pl.multiple_of(t * tile, 128), tile)
        full = mult[taken, span].astype(jnp.float32) + penalty * resid
        return full.astype(jnp.bfloat16), tiles_of, span

    def pair_tiles(first, last):
        @pl.loop(first, last)
        def _(t):
            weight, tiles_of, span = weighted(0, t, mult_q, shift_value, every)
            for part in range(col_groups):
                left = tiles_of[part][:, : depth // 2]
                right = tiles_of[part][:, depth // 2 :]
                pair_acc[part, :, : depth // 2] += jnp.dot(
                    ham[:, span], left, preferred_element_type=jnp.float32
                ) - jnp.dot(weight, left, preferred_element_type=jnp.float32)
                pair_acc[part, :, depth // 2 :] -= jnp.dot(
                    weight, right, preferred_element_type=jnp.float32
                )

    def ph_tiles(shift, taken):
        @pl.loop(0, tiles)
        def _(t):
            weight, tiles_of, _span = weighted(1, t, mult_g, shift[taken], taken)
            for part in range(col_groups):
                ph_acc[part, taken] -= jnp.dot(
                    weight, tiles_of[part], preferred_element_type=jnp.float32
                )

    fetches = [
        pltpu.make_async_copy(mult_q_hbm, mult_q, fetch_sem.at[0]),
        pltpu.make_async_copy(ham_hbm, ham, fetch_sem.at[1]),
        pltpu.make_async_copy(mult_g_hbm, mult_g, fetch_sem.at[2]),
    ]
    lag = min(2, half)

    launch(0)
    place(1)
    for fetch in fetches:
        fetch.start()
    pair_acc[...] = jnp.zeros_like(pair_acc)
    ph_acc[...] = jnp.zeros_like(ph_acc)
    for step in range(1, half + 1):
        arrive(0, step)
        if step == 1:
            lend(0)
        if step == lag:
            launch(1)
            lend(1)
        if step > lag:
            arrive(1, step - lag)
    settle(0)
    fetches[0].wait()
    fetches[1].wait()
    for k in range(lag):
        pair_tiles(tiles * k // lag, tiles * (k + 1) // lag)
        arrive(1, half - lag + 1 + k)
    for d in range(1, col_groups):
        swapping(0, d, 0, every).start()

    for d in range(1, col_groups):
        stats_over(d, col).wait_send()
    for d in range(1, groups):
        stats_rows(d, (row + groups - d) % groups).wait_recv()
        stats_rows(d, row).wait_send()
    sums = jnp.sum(stats_all[...].reshape((groups * col_groups,) + stats_ref.shape), axis=0)
    sums_out[...] = sums
    means = 2.0 * sums[0:1] / lengths_ref[0:1]
    shift = jnp.sum(member_ref[...] * means, axis=1, keepdims=True)

    settle(1)
    fetches[2].wait()
    for h in range(2):
        ph_tiles(shift, halves[h])
        if h == 0:
            drain(0)
        else:
            finish(0, pair_out, 0, every)
        for d in range(1, col_groups):
            swapping(1, d, 1 + h, halves[h]).start()
    drain(1)
    for h in range(2):
        finish(1, ph_out, 1 + h, halves[h])
    for d in range(1, col_groups):
        swapping(0, d, 0, every).wait_send()
        for h in range(2):
            swapping(1, d, 1 + h, halves[h]).wait_send()


def spread(groups, col_groups, pair_local, ph_local, stats, member, lengths, ham, mult_q, mult_g):
    block, depth = pair_local.shape
    half = groups // 4
    over = max(col_groups - 1, 1)
    dma = pltpu.SemaphoreType.DMA
    kind = pair_local.dtype
    grad = jax.ShapeDtypeStruct((block, depth), jnp.float32)
    vmem = pl.BlockSpec(memory_space=pltpu.VMEM)
    hbm = pl.BlockSpec(memory_space=pl.ANY)
    return pl.pallas_call(
        functools.partial(spread_kernel, groups, col_groups),
        name="spread",
        out_shape=(grad, grad, jax.ShapeDtypeStruct(stats.shape, stats.dtype)),
        in_specs=[vmem] * 5 + [hbm] * 3,
        out_specs=(vmem,) * 3,
        scratch_shapes=[
            pltpu.VMEM((groups, block, depth), kind),
            pltpu.VMEM((groups, block, depth), kind),
            pltpu.VMEM((col_groups, block, depth), kind),
            pltpu.VMEM((col_groups, block, depth), kind),
            pltpu.VMEM((groups, col_groups) + stats.shape, stats.dtype),
            pltpu.VMEM(ham.shape, ham.dtype),
            pltpu.VMEM(mult_q.shape, mult_q.dtype),
            pltpu.VMEM(mult_g.shape, mult_g.dtype),
            pltpu.VMEM((col_groups, block, depth), jnp.float32),
            pltpu.VMEM((col_groups, block, depth), jnp.float32),
            pltpu.VMEM((over, block, depth), jnp.float32),
            pltpu.VMEM((over, block, depth), jnp.float32),
            dma((2,)),
            dma((2,)),
            dma((2, over)),
            dma((2, over)),
            dma((2, 2, half)),
            dma((2, 2, half)),
            dma((2, 2, half + 1)),
            dma((2, 2, half + 1)),
            dma((2, 3)),
            dma((over,)),
            dma((over,)),
            dma((groups - 1,)),
            dma((groups - 1,)),
            dma((3,)),
            dma((3, over)),
            dma((3, over)),
        ],
        compiler_params=pltpu.CompilerParams(
            collective_id=0, has_side_effects=True, vmem_limit_bytes=56 << 20
        ),
    )(pair_local, ph_local, stats, member, lengths, ham, mult_q, mult_g)


def select(one_hot, values, left_axis):
    if values.dtype == jnp.float32:
        precision = lax.Precision.HIGHEST
    else:
        precision = None
    return lax.dot_general(
        one_hot.astype(values.dtype),
        values,
        (((left_axis,), (0,)), ((), ())),
        precision=precision,
        preferred_element_type=jnp.float32,
    ).astype(values.dtype)


def local(
    density_factor,
    hole_factor,
    ph_factor,
    hamiltonian,
    multiplier_q,
    multiplier_g,
    ph_perm,
    block_lengths,
):
    groups = lax.axis_size("row")
    col_groups = lax.axis_size("col")
    row_index = lax.axis_index("row")
    col_index = lax.axis_index("col")
    block, rank_part = density_factor.shape
    width = multiplier_q.shape[1]
    sends = block // groups
    pair_local = jnp.concatenate([density_factor, hole_factor], axis=1)

    index = jnp.arange(block, dtype=jnp.int32)
    row_ids = row_index * block + index
    mine = lax.dynamic_slice_in_dim(ph_perm, row_index * block, block)
    source = mine // block
    same_source = (source[:, None] == source[None, :]) & (index[None, :] < index[:, None])
    slot = source * sends + jnp.sum(same_source.astype(jnp.int32), axis=1)
    everywhere = jnp.arange(groups * block, dtype=jnp.int32)
    inverse = jnp.sum(
        jnp.where(ph_perm[None, :] == row_ids[:, None], everywhere[None, :], 0), axis=1
    )
    target = inverse // block
    same_target = (target[:, None] == target[None, :]) & (inverse[None, :] < inverse[:, None])
    outlet = target * sends + jnp.sum(same_target.astype(jnp.int32), axis=1)
    send_hot = outlet[:, None] == index[None, :]
    take_hot = slot[:, None] == index[None, :]

    outgoing = select(send_hot, density_factor, 0)
    incoming = lax.all_to_all(outgoing, "row", split_axis=0, concat_axis=0, tiled=True)
    density_ph = select(take_hot, incoming, 1)
    ph_local = jnp.concatenate([density_ph, ph_factor], axis=1)

    lengths = block_lengths.astype(jnp.float32)
    count = block_lengths.shape[0]
    upto = jnp.arange(count, dtype=jnp.int32)
    ends = jnp.sum(jnp.where(upto[None, :] <= upto[:, None], block_lengths[None, :], 0), axis=1)
    starts = ends - block_lengths

    def member_of(ids):
        inside = (ids[:, None] >= starts[None, :]) & (ids[:, None] < ends[None, :])
        return inside.astype(jnp.float32)

    member = member_of(row_ids)
    member_ph = member_of(mine)
    density_sq = jnp.sum(jnp.square(density_factor.astype(jnp.float32)), axis=1)
    ph_sq = jnp.sum(jnp.square(ph_factor.astype(jnp.float32)), axis=1)
    offset = row_index * block - col_index * width
    holds = (offset >= 0) & (offset < width)
    square = lax.dynamic_slice_in_dim(
        multiplier_g, jnp.clip(offset, 0, width - block), block, axis=1
    )
    keep = (index[:, None] == index[None, :]) & holds
    mult_diag = jnp.sum(jnp.where(keep, square.astype(jnp.float32), 0.0), axis=1)
    sums = jnp.stack(
        [
            jnp.sum(member * density_sq[:, None], axis=0),
            jnp.sum(member_ph * (mult_diag - penalty * ph_sq)[:, None], axis=0),
        ]
    )
    stats = jnp.pad(sums, ((0, 6), (0, -count % 128)))
    lanes = ((0, 0), (0, -count % 128))
    pair_grad, ph_grad, sums = spread(
        groups,
        col_groups,
        pair_local,
        ph_local,
        stats,
        jnp.pad(member_ph, lanes),
        jnp.pad(jnp.broadcast_to(lengths, (8, count)), lanes, constant_values=1.0),
        hamiltonian,
        multiplier_q,
        multiplier_g,
    )
    sums = sums[:, :count]
    scale_means = 2.0 * (sums[1] + penalty * sums[0]) / lengths
    scale_rows = jnp.sum(member * scale_means[None, :], axis=1)

    back = select(take_hot, ph_grad[:, :rank_part], 0)
    back = lax.all_to_all(back, "row", split_axis=0, concat_axis=0, tiled=True)
    returned = select(send_hot, back, 1)
    grad_density = (
        pair_grad[:, :rank_part]
        + 2.0 * scale_rows[:, None] * density_factor.astype(jnp.float32)
        + returned
    )
    grad_hole = pair_grad[:, rank_part:]
    grad_ph = ph_grad[:, rank_part:]
    return (grad_density, grad_hole, grad_ph)


def solution(mesh):
    return jax.shard_map(
        local,
        mesh=mesh,
        in_specs=(
            P("row", "col"),
            P("row", "col"),
            P("row", "col"),
            P("row", "col"),
            P("row", "col"),
            P("row", "col"),
            P(),
            P(),
        ),
        out_specs=(P("row", "col"), P("row", "col"), P("row", "col")),
        check_vma=False,
    )
```

```python
import functools

import jax
import jax.numpy as jnp
from jax import lax
from jax.experimental import pallas as pl
from jax.experimental.pallas import tpu as pltpu
from jax.sharding import PartitionSpec as P

shift_value = 2.0
penalty = 2.5


MESH = pl.DeviceIdType.MESH


def spread_kernel(
    groups,
    col_groups,
    pair_ref,
    ph_ref,
    stats_ref,
    member_ref,
    lengths_ref,
    ham_hbm,
    mult_q_hbm,
    mult_g_hbm,
    pair_out,
    ph_out,
    sums_out,
    pair_cols,
    ph_cols,
    pair_own,
    ph_own,
    stats_all,
    ham,
    mult_q,
    mult_g,
    pair_acc,
    ph_acc,
    pair_in,
    ph_in,
    place_send,
    place_recv,
    own_send,
    own_recv,
    ring_send,
    ring_recv,
    mate_send,
    mate_recv,
    here_sem,
    stats_send,
    stats_recv,
    rows_send,
    rows_recv,
    fetch_sem,
    swap_send,
    swap_recv,
):
    row = lax.axis_index("row")
    col = lax.axis_index("col")
    per = groups // col_groups
    chips = groups // 2
    half = chips // 2
    block = pair_ref.shape[0]
    core = row % 2
    chip = row // 2
    pos = jnp.where(chip % 2 == 0, chip // 2, chips - 1 - chip // 2)

    def row_at(place, which):
        place = (place + chips) % chips
        return jnp.where(place < half, 2 * place, 2 * (chips - 1 - place) + 1) * 2 + which

    ring_to = [(row_at(pos + 1, core), col), (row_at(pos - 1, core), col)]
    mate = (row + 1 - 2 * core, col)
    home = row // per
    moved = col != home
    partner = (col * per + row % per, home)
    peers = [(row, (col + d) % col_groups) for d in range(1, col_groups)]

    others = [(row + d) % groups for d in range(1, groups)]

    barrier = pltpu.get_barrier_semaphore()
    for device in [(other, col) for other in others] + peers:
        pl.semaphore_signal(barrier, inc=1, device_id=device, device_id_type=MESH)

    @pl.when(moved)
    def _():
        pl.semaphore_signal(barrier, inc=1, device_id=partner, device_id_type=MESH)

    greeted = len(others) + len(peers)
    pl.semaphore_wait(barrier, jnp.where(moved, greeted + 1, greeted))

    locals_ = [pair_ref, ph_ref]
    cols_ = [pair_cols, ph_cols]
    owns_ = [pair_own, ph_own]

    def placing(a):
        return pltpu.make_async_remote_copy(
            src_ref=locals_[a],
            dst_ref=cols_[a].at[partner[0]],
            send_sem=place_send.at[a],
            recv_sem=place_recv.at[a],
            device_id=partner,
            device_id_type=MESH,
        )

    def staying(a):
        return pltpu.make_async_copy(locals_[a], cols_[a].at[row], here_sem.at[a, 0])

    def keeping(a):
        return pltpu.make_async_copy(locals_[a], owns_[a].at[col], here_sem.at[a, 1])

    def owning(a, d, origin):
        return pltpu.make_async_remote_copy(
            src_ref=locals_[a],
            dst_ref=owns_[a].at[origin],
            send_sem=own_send.at[a, d - 1],
            recv_sem=own_recv.at[a, d - 1],
            device_id=peers[d - 1],
            device_id_type=MESH,
        )

    def piece(a, slot, way, step):
        if step == half:
            return cols_[a].at[slot, pl.ds(way * (block // 2), block // 2)]
        return cols_[a].at[slot]

    def ring(a, way, step, travelled):
        sign = -1 if way == 0 else 1
        ref = piece(a, row_at(pos + sign * travelled, core), way, step)
        return pltpu.make_async_remote_copy(
            src_ref=ref,
            dst_ref=ref,
            send_sem=ring_send.at[a, way, step - 1],
            recv_sem=ring_recv.at[a, way, step - 1],
            device_id=ring_to[way],
            device_id_type=MESH,
        )

    def mating(a, way, step, which):
        sign = -1 if way == 0 else 1
        ref = piece(a, row_at(pos + sign * step, which), way, step)
        return pltpu.make_async_remote_copy(
            src_ref=ref,
            dst_ref=ref,
            send_sem=mate_send.at[a, way, step],
            recv_sem=mate_recv.at[a, way, step],
            device_id=mate,
            device_id_type=MESH,
        )

    def stats_here():
        return pltpu.make_async_copy(stats_ref, stats_all.at[row, col], here_sem.at[0, 2])

    def stats_over(d, origin):
        return pltpu.make_async_remote_copy(
            src_ref=stats_ref,
            dst_ref=stats_all.at[row, origin],
            send_sem=stats_send.at[d - 1],
            recv_sem=stats_recv.at[d - 1],
            device_id=peers[d - 1],
            device_id_type=MESH,
        )

    def stats_rows(d, origin):
        return pltpu.make_async_remote_copy(
            src_ref=stats_all.at[origin],
            dst_ref=stats_all.at[origin],
            send_sem=rows_send.at[d - 1],
            recv_sem=rows_recv.at[d - 1],
            device_id=(others[d - 1], col),
            device_id_type=MESH,
        )

    stats_here().start()
    for d in range(1, col_groups):
        stats_over(d, col).start()
    def place(a):
        @pl.when(moved)
        def _():
            placing(a).start()

        @pl.when(jnp.logical_not(moved))
        def _():
            staying(a).start()

        keeping(a).start()

    place(0)
    place(1)

    stats_here().wait()
    for d in range(1, col_groups):
        stats_over(d, (col + col_groups - d) % col_groups).wait_recv()
    for d in range(1, groups):
        stats_rows(d, row).start()

    def launch(a):
        @pl.when(moved)
        def _():
            placing(a).wait_recv()

        @pl.when(jnp.logical_not(moved))
        def _():
            staying(a).wait()

        for way in range(2):
            ring(a, way, 1, 0).start()
        mating(a, 0, 0, core).start()

    def lend(a):
        for d in range(1, col_groups):
            owning(a, d, col).start()

    def arrive(a, step):
        for way in range(2):
            ring(a, way, step, step).wait_recv()
            if step < half:
                ring(a, way, step + 1, step).start()
            mating(a, way, step, core).start()

    def settle(a):
        mating(a, 0, 0, 1 - core).wait_recv()
        for step in range(1, half + 1):
            for way in range(2):
                mating(a, way, step, 1 - core).wait_recv()
        for d in range(1, col_groups):
            owning(a, d, (col + col_groups - d) % col_groups).wait_recv()
        keeping(a).wait()

    def drain(a):
        mating(a, 0, 0, core).wait_send()
        for step in range(1, half + 1):
            for way in range(2):
                mating(a, way, step, core).wait_send()
                ring(a, way, step, step - 1).wait_send()
        for d in range(1, col_groups):
            owning(a, d, col).wait_send()

        @pl.when(moved)
        def _():
            placing(a).wait_send()

    accs_ = [pair_acc, ph_acc]
    ins_ = [pair_in, ph_in]

    every = slice(0, block)
    halves = [slice(0, block // 2), slice(block // 2, block)]

    def swapping(a, d, slot, rows):
        return pltpu.make_async_remote_copy(
            src_ref=accs_[a].at[(col + d) % col_groups, rows],
            dst_ref=ins_[a].at[d - 1, rows],
            send_sem=swap_send.at[slot, d - 1],
            recv_sem=swap_recv.at[slot, d - 1],
            device_id=peers[d - 1],
            device_id_type=MESH,
        )

    def finish(a, out, slot, rows):
        total = accs_[a][col, rows]
        for d in range(1, col_groups):
            swapping(a, d, slot, rows).wait_recv()
            total = total + ins_[a][d - 1, rows]
        out[rows] = 2.0 * total

    depth = pair_ref.shape[1]
    joined = 2 if per % 2 == 0 else 1
    tile = joined * block
    tiles = per // joined
    offset = row * block - col * per * block

    def weighted(a, t, mult, shift, taken):
        gram = None
        tiles_of = []
        for part in range(col_groups):
            there = cols_[a][pl.ds(part * per + t * joined, joined)].reshape(tile, depth)
            tiles_of.append(there)
            term = lax.dot_general(
                owns_[a][part, taken],
                there,
                (((1,), (1,)), ((), ())),
                preferred_element_type=jnp.float32,
            )
            gram = term if gram is None else gram + term
        dims = (taken.stop - taken.start, tile)
        rows = lax.broadcasted_iota(jnp.int32, dims, 0) + (offset + taken.start)
        places = lax.broadcasted_iota(jnp.int32, dims, 1) + t * tile
        resid = jnp.where(rows == places, shift, 0.0) - gram
        span = pl.ds(pl.multiple_of(t * tile, 128), tile)
        full = mult[taken, span].astype(jnp.float32) + penalty * resid
        return full.astype(jnp.bfloat16), tiles_of, span

    def pair_tiles(first, last):
        @pl.loop(first, last)
        def _(t):
            weight, tiles_of, span = weighted(0, t, mult_q, shift_value, every)
            for part in range(col_groups):
                left = tiles_of[part][:, : depth // 2]
                right = tiles_of[part][:, depth // 2 :]
                pair_acc[part, :, : depth // 2] += jnp.dot(
                    ham[:, span], left, preferred_element_type=jnp.float32
                ) - jnp.dot(weight, left, preferred_element_type=jnp.float32)
                pair_acc[part, :, depth // 2 :] -= jnp.dot(
                    weight, right, preferred_element_type=jnp.float32
                )

    def ph_tiles(shift, taken):
        @pl.loop(0, tiles)
        def _(t):
            weight, tiles_of, _span = weighted(1, t, mult_g, shift[taken], taken)
            for part in range(col_groups):
                ph_acc[part, taken] -= jnp.dot(
                    weight, tiles_of[part], preferred_element_type=jnp.float32
                )

    fetches = [
        pltpu.make_async_copy(mult_q_hbm, mult_q, fetch_sem.at[0]),
        pltpu.make_async_copy(ham_hbm, ham, fetch_sem.at[1]),
        pltpu.make_async_copy(mult_g_hbm, mult_g, fetch_sem.at[2]),
    ]
    lag = 1

    launch(0)
    for fetch in fetches:
        fetch.start()
    pair_acc[...] = jnp.zeros_like(pair_acc)
    ph_acc[...] = jnp.zeros_like(ph_acc)
    for step in range(1, half + 1):
        arrive(0, step)
        if step == 1:
            lend(0)
        if step == lag:
            launch(1)
            lend(1)
        if step > lag:
            arrive(1, step - lag)
    settle(0)
    fetches[0].wait()
    fetches[1].wait()
    for k in range(lag):
        pair_tiles(tiles * k // lag, tiles * (k + 1) // lag)
        arrive(1, half - lag + 1 + k)
    for d in range(1, col_groups):
        swapping(0, d, 0, every).start()

    for d in range(1, col_groups):
        stats_over(d, col).wait_send()
    for d in range(1, groups):
        stats_rows(d, (row + groups - d) % groups).wait_recv()
        stats_rows(d, row).wait_send()
    sums = jnp.sum(stats_all[...].reshape((groups * col_groups,) + stats_ref.shape), axis=0)
    sums_out[...] = sums
    means = 2.0 * sums[0:1] / lengths_ref[0:1]
    shift = jnp.sum(member_ref[...] * means, axis=1, keepdims=True)

    settle(1)
    fetches[2].wait()
    for h in range(2):
        ph_tiles(shift, halves[h])
        if h == 0:
            drain(0)
        else:
            finish(0, pair_out, 0, every)
        for d in range(1, col_groups):
            swapping(1, d, 1 + h, halves[h]).start()
    drain(1)
    for h in range(2):
        finish(1, ph_out, 1 + h, halves[h])
    for d in range(1, col_groups):
        swapping(0, d, 0, every).wait_send()
        for h in range(2):
            swapping(1, d, 1 + h, halves[h]).wait_send()


def spread(groups, col_groups, pair_local, ph_local, stats, member, lengths, ham, mult_q, mult_g):
    block, depth = pair_local.shape
    half = groups // 4
    over = max(col_groups - 1, 1)
    dma = pltpu.SemaphoreType.DMA
    kind = pair_local.dtype
    grad = jax.ShapeDtypeStruct((block, depth), jnp.float32)
    vmem = pl.BlockSpec(memory_space=pltpu.VMEM)
    hbm = pl.BlockSpec(memory_space=pl.ANY)
    return pl.pallas_call(
        functools.partial(spread_kernel, groups, col_groups),
        name="spread",
        out_shape=(grad, grad, jax.ShapeDtypeStruct(stats.shape, stats.dtype)),
        in_specs=[vmem] * 5 + [hbm] * 3,
        out_specs=(vmem,) * 3,
        scratch_shapes=[
            pltpu.VMEM((groups, block, depth), kind),
            pltpu.VMEM((groups, block, depth), kind),
            pltpu.VMEM((col_groups, block, depth), kind),
            pltpu.VMEM((col_groups, block, depth), kind),
            pltpu.VMEM((groups, col_groups) + stats.shape, stats.dtype),
            pltpu.VMEM(ham.shape, ham.dtype),
            pltpu.VMEM(mult_q.shape, mult_q.dtype),
            pltpu.VMEM(mult_g.shape, mult_g.dtype),
            pltpu.VMEM((col_groups, block, depth), jnp.float32),
            pltpu.VMEM((col_groups, block, depth), jnp.float32),
            pltpu.VMEM((over, block, depth), jnp.float32),
            pltpu.VMEM((over, block, depth), jnp.float32),
            dma((2,)),
            dma((2,)),
            dma((2, over)),
            dma((2, over)),
            dma((2, 2, half)),
            dma((2, 2, half)),
            dma((2, 2, half + 1)),
            dma((2, 2, half + 1)),
            dma((2, 3)),
            dma((over,)),
            dma((over,)),
            dma((groups - 1,)),
            dma((groups - 1,)),
            dma((3,)),
            dma((3, over)),
            dma((3, over)),
        ],
        compiler_params=pltpu.CompilerParams(
            collective_id=0, has_side_effects=True, vmem_limit_bytes=56 << 20
        ),
    )(pair_local, ph_local, stats, member, lengths, ham, mult_q, mult_g)


def select(one_hot, values, left_axis):
    if values.dtype == jnp.float32:
        precision = lax.Precision.HIGHEST
    else:
        precision = None
    return lax.dot_general(
        one_hot.astype(values.dtype),
        values,
        (((left_axis,), (0,)), ((), ())),
        precision=precision,
        preferred_element_type=jnp.float32,
    ).astype(values.dtype)


def local(
    density_factor,
    hole_factor,
    ph_factor,
    hamiltonian,
    multiplier_q,
    multiplier_g,
    ph_perm,
    block_lengths,
):
    groups = lax.axis_size("row")
    col_groups = lax.axis_size("col")
    row_index = lax.axis_index("row")
    col_index = lax.axis_index("col")
    block, rank_part = density_factor.shape
    width = multiplier_q.shape[1]
    sends = block // groups
    pair_local = jnp.concatenate([density_factor, hole_factor], axis=1)

    index = jnp.arange(block, dtype=jnp.int32)
    row_ids = row_index * block + index
    mine = lax.dynamic_slice_in_dim(ph_perm, row_index * block, block)
    source = mine // block
    same_source = (source[:, None] == source[None, :]) & (index[None, :] < index[:, None])
    slot = source * sends + jnp.sum(same_source.astype(jnp.int32), axis=1)
    everywhere = jnp.arange(groups * block, dtype=jnp.int32)
    inverse = jnp.sum(
        jnp.where(ph_perm[None, :] == row_ids[:, None], everywhere[None, :], 0), axis=1
    )
    target = inverse // block
    same_target = (target[:, None] == target[None, :]) & (inverse[None, :] < inverse[:, None])
    outlet = target * sends + jnp.sum(same_target.astype(jnp.int32), axis=1)
    send_hot = outlet[:, None] == index[None, :]
    take_hot = slot[:, None] == index[None, :]

    outgoing = select(send_hot, density_factor, 0)
    incoming = lax.all_to_all(outgoing, "row", split_axis=0, concat_axis=0, tiled=True)
    density_ph = select(take_hot, incoming, 1)
    ph_local = jnp.concatenate([density_ph, ph_factor], axis=1)

    lengths = block_lengths.astype(jnp.float32)
    count = block_lengths.shape[0]
    upto = jnp.arange(count, dtype=jnp.int32)
    ends = jnp.sum(jnp.where(upto[None, :] <= upto[:, None], block_lengths[None, :], 0), axis=1)
    starts = ends - block_lengths

    def member_of(ids):
        inside = (ids[:, None] >= starts[None, :]) & (ids[:, None] < ends[None, :])
        return inside.astype(jnp.float32)

    member = member_of(row_ids)
    member_ph = member_of(mine)
    density_sq = jnp.sum(jnp.square(density_factor.astype(jnp.float32)), axis=1)
    ph_sq = jnp.sum(jnp.square(ph_factor.astype(jnp.float32)), axis=1)
    offset = row_index * block - col_index * width
    holds = (offset >= 0) & (offset < width)
    square = lax.dynamic_slice_in_dim(
        multiplier_g, jnp.clip(offset, 0, width - block), block, axis=1
    )
    keep = (index[:, None] == index[None, :]) & holds
    mult_diag = jnp.sum(jnp.where(keep, square.astype(jnp.float32), 0.0), axis=1)
    sums = jnp.stack(
        [
            jnp.sum(member * density_sq[:, None], axis=0),
            jnp.sum(member_ph * (mult_diag - penalty * ph_sq)[:, None], axis=0),
        ]
    )
    stats = jnp.pad(sums, ((0, 6), (0, -count % 128)))
    lanes = ((0, 0), (0, -count % 128))
    pair_grad, ph_grad, sums = spread(
        groups,
        col_groups,
        pair_local,
        ph_local,
        stats,
        jnp.pad(member_ph, lanes),
        jnp.pad(jnp.broadcast_to(lengths, (8, count)), lanes, constant_values=1.0),
        hamiltonian,
        multiplier_q,
        multiplier_g,
    )
    sums = sums[:, :count]
    scale_means = 2.0 * (sums[1] + penalty * sums[0]) / lengths
    scale_rows = jnp.sum(member * scale_means[None, :], axis=1)

    back = select(take_hot, ph_grad[:, :rank_part], 0)
    back = lax.all_to_all(back, "row", split_axis=0, concat_axis=0, tiled=True)
    returned = select(send_hot, back, 1)
    grad_density = (
        pair_grad[:, :rank_part]
        + 2.0 * scale_rows[:, None] * density_factor.astype(jnp.float32)
        + returned
    )
    grad_hole = pair_grad[:, rank_part:]
    grad_ph = ph_grad[:, rank_part:]
    return (grad_density, grad_hole, grad_ph)


def solution(mesh):
    return jax.shard_map(
        local,
        mesh=mesh,
        in_specs=(
            P("row", "col"),
            P("row", "col"),
            P("row", "col"),
            P("row", "col"),
            P("row", "col"),
            P("row", "col"),
            P(),
            P(),
        ),
        out_specs=(P("row", "col"), P("row", "col"), P("row", "col")),
        check_vma=False,
    )
```
